128 devices in a mesh: dp: 8 (over z, core), tensor: 16 (over y, x).
Axes of the slice: x: 4, y: 4, z: 4, core: 2. Of those that a mesh axis runs over, the one named last changes fastest.
Arguments:
- residues: bfloat16 [4096, 1024], P('dp'), may hold values from -40 to 40
- block_protein: int32 [32], P('dp'), may hold values from 0 to 31, as said below
- protein_length: int32 [32], replicated, may hold values from 0 to 256, as said below
- decoder_group: int32 [32], replicated, may hold values from 0 to 7, as said below
- enc_gain: float32 [1024], replicated, may hold values from 0.1 to 1.9
- enc_query: bfloat16 [1024, 16384], P(None, 'tensor'), may hold values from -2 to 2
- enc_key: bfloat16 [1024, 16384], P(None, 'tensor'), may hold values from -2 to 2
- enc_value: bfloat16 [1024, 16384], P(None, 'tensor'), may hold values from -0.1875 to 0.1875
- enc_out: bfloat16 [16384, 1024], P('tensor'), may hold values from -0.1875 to 0.1875
- decoder_states: bfloat16 [3072, 1024], P('dp'), may hold values from -40 to 40
- query_protein: int32 [3072], P('dp'), may hold values from 0 to 31, as said below
- dec_gain: float32 [1024], replicated, may hold values from 0.1 to 1.9
- final_gain: float32 [1024], replicated, may hold values from 0.1 to 1.9
- cross_query: bfloat16 [1024, 16384], P(None, 'tensor'), may hold values from -2 to 2
- cross_key: bfloat16 [1024, 16384], P(None, 'tensor'), may hold values from -2 to 2
- cross_value: bfloat16 [1024, 16384], P(None, 'tensor'), may hold values from -0.1875 to 0.1875
- cross_out: bfloat16 [16384, 1024], P('tensor'), may hold values from -0.1875 to 0.1875
Outputs:
- encoded: bfloat16 [4096, 1024], P('dp', 'tensor')
- decoded: bfloat16 [3072, 1024], P(('dp', 'tensor'))
The draws below stay inside these ranges and needn't reach their ends.
Inputs may be any that keep to these rules, and one draw needn't show every extreme that they name: `block_protein`: block b of dp group d names a protein id from d * 4 to (d + 1) * 4 - 1; the blocks of one protein are consecutive and the ids rise along a group's blocks. `protein_length`: A protein of n blocks has a length from (n - 1) * 128 + 1 to n * 128; an id that no block names has length 0; no protein spans more than 2 blocks. `decoder_group`: at most 2 blocks of one dp group belong to proteins of one decoder group, and in every draw some decoder group gets exactly 2 blocks from every dp group; every decoder group owns a protein of positive length. `query_protein`: query row i names a protein of positive length whose decoder group is i // 384.
All inputs are finite; a program needn't handle non-finite values.
Results may differ from the reference program's by a relative error of at most 0.017.
Values may be sent and summed in bfloat16 or wider, within the bound.
No kernel may reach another device: no remote copies, remote signals or barrier semaphores. Data moves between devices by JAX's collectives and lax.ppermute only.
A program may use at most 128 MiB of HBM per device.

```python
import jax
import jax.numpy as jnp
from jax import lax

D = 1024
HEAD_DIM = 128
BLOCK = 128
BLK_DEV = 4
Q_DEV = 384
HEADS = 128
SLOTS = 2
TOKENS = 4096
QROWS = 3072
PROTEINS = 32
N_DP = 8


def layout(key):
    base = jax.random.fold_in(key, 101)
    hot = jax.random.randint(jax.random.fold_in(base, 1), (), 0, N_DP)
    flip = jax.random.randint(jax.random.fold_in(base, 2), (N_DP,), 0, 2)
    cuts = jax.random.randint(jax.random.fold_in(base, 3), (N_DP, BLK_DEV), 0, 2)
    column = jnp.arange(BLK_DEV, dtype=jnp.int32)
    device = jnp.arange(N_DP, dtype=jnp.int32)[:, None]
    joined = (device == 0) & (column[None, :] < SLOTS)
    starts = jnp.where((column[None, :] == 0) | (column[None, :] == SLOTS), 1, jnp.where(joined, 0, cuts))
    local = jnp.cumsum(starts, axis=1).astype(jnp.int32) - 1
    block_ids = device * BLK_DEV + local
    in_hot = (column[None, :] < SLOTS) == (flip[:, None] == 0)
    other_start = jnp.where(flip == 0, SLOTS, 0)
    first_local = jnp.sum(jnp.where(column[None, :] == other_start[:, None], local, 0), axis=1)
    random_pick = jax.random.randint(jax.random.fold_in(base, 4), (N_DP, BLK_DEV), 0, N_DP - 1)
    picked = jnp.take_along_axis(random_pick, local, axis=1)
    spread = jnp.where(local == first_local[:, None], device % (N_DP - 1), picked)
    dest = jnp.where(in_hot, hot, (hot + 1 + spread) % N_DP)
    target = jnp.arange(BLK_DEV, dtype=jnp.int32)
    match = local[:, None, :] == target[None, :, None]
    present = jnp.any(match, axis=2)
    owned = jnp.sum(match.astype(jnp.int32), axis=2)
    group_of = jnp.max(jnp.where(match, dest[:, None, :], -1), axis=2)
    filler = jax.random.randint(jax.random.fold_in(base, 5), (N_DP, BLK_DEV), 0, N_DP)
    groups = jnp.where(present, group_of, filler).reshape(-1)
    tail = jax.random.randint(jax.random.fold_in(base, 6), (N_DP, BLK_DEV), 1, BLOCK + 1)
    full_one = (device == 0) & (target[None, :] == 0)
    tail = jnp.where(full_one, BLOCK, tail)
    lengths = jnp.where(present, (owned - 1) * BLOCK + tail, 0).reshape(-1)
    candidate = (groups[None, :] == jnp.arange(N_DP, dtype=jnp.int32)[:, None]) & (lengths[None, :] > 0)
    counted = jnp.sum(candidate.astype(jnp.int32), axis=1)
    row_group = jnp.arange(QROWS, dtype=jnp.int32) // Q_DEV
    choose = jax.random.randint(jax.random.fold_in(base, 7), (QROWS,), 0, counted[row_group])
    running = jnp.cumsum(candidate.astype(jnp.int32), axis=1)
    select = candidate[row_group] & (running[row_group] == choose[:, None] + 1)
    ids = jnp.arange(PROTEINS, dtype=jnp.int32)
    queries = jnp.sum(jnp.where(select, ids[None, :], 0), axis=1).astype(jnp.int32)
    return (block_ids.reshape(-1).astype(jnp.int32), lengths.astype(jnp.int32), groups.astype(jnp.int32), queries)


def draw_block_protein(key, part):
    return layout(key)[0]


def draw_protein_length(key, part):
    return layout(key)[1]


def draw_decoder_group(key, part):
    return layout(key)[2]


def draw_query_protein(key, part):
    return layout(key)[3]


def states_draw(key, salt, rows):
    noise = jax.random.normal(jax.random.fold_in(key, salt), (rows, D), jnp.float32)
    return noise.astype(jnp.bfloat16)


def draw_residues(key, part):
    return states_draw(key, 31, TOKENS)


def draw_decoder_states(key, part):
    return states_draw(key, 41, QROWS)


def projection(key, salt, second):
    shape = (D, HEADS * HEAD_DIM)
    return jnp.clip(jax.random.normal(jax.random.fold_in(key, salt + 10 + second), shape, jnp.float32) * D ** (-0.5), -1.9, 1.9).astype(jnp.bfloat16)


def draw_enc_query(key, part):
    return projection(key, 200, 0)


def draw_enc_key(key, part):
    return projection(key, 200, 1)


def draw_cross_query(key, part):
    return projection(key, 300, 0)


def draw_cross_key(key, part):
    return projection(key, 300, 1)


def shard_levels(stream_key, extent, shards, low, high):
    def one(axis_at, shards_of):
        heights = jax.random.uniform(jax.random.fold_in(jax.random.fold_in(stream_key, 6), axis_at), (shards_of,), jnp.float32, low / len(shards), high / len(shards))
        return jnp.repeat(jnp.exp(heights), extent[axis_at] // shards_of).reshape((-1,) + (1,) * (len(extent) - axis_at - 1))

    level = one(*shards[0])
    for cut in shards[1:]:
        level = level * one(*cut)
    return level


def centred(key, extent, deviation, limit, split=(), kind=jnp.bfloat16):
    entries = deviation * jax.random.normal(key, extent, jnp.float32)
    if split:
        entries = entries * shard_levels(key, extent, split, -0.22, 0.18)
    return jnp.clip(entries, -limit, limit).astype(kind)


def setup_inputs(seed: int = 0) -> dict:
    arg_keys = jax.random.split(jax.random.key(seed), 18)
    return {
        "residues": draw_residues(jax.random.fold_in(arg_keys[17], 71), 0),
        "block_protein": draw_block_protein(jax.random.fold_in(arg_keys[17], 71), 0),
        "protein_length": draw_protein_length(jax.random.fold_in(arg_keys[17], 71), 0),
        "decoder_group": draw_decoder_group(jax.random.fold_in(arg_keys[17], 71), 0),
        "enc_gain": jnp.clip(1.0 + 0.18 * jax.random.normal(arg_keys[4], (D,), jnp.float32), 0.1, 1.9),
        "enc_query": draw_enc_query(jax.random.fold_in(arg_keys[17], 71), 0),
        "enc_key": draw_enc_key(jax.random.fold_in(arg_keys[17], 71), 0),
        "enc_value": centred(arg_keys[7], (D, HEADS * HEAD_DIM), D ** -0.5, 0.1875, ((1, 16),)),
        "enc_out": centred(arg_keys[8], (HEADS * HEAD_DIM, D), (8 * HEAD_DIM) ** -0.5, 0.1875, ((0, 16),)),
        "decoder_states": draw_decoder_states(jax.random.fold_in(arg_keys[17], 71), 0),
        "query_protein": draw_query_protein(jax.random.fold_in(arg_keys[17], 71), 0),
        "dec_gain": jnp.clip(1.0 + 0.18 * jax.random.normal(arg_keys[11], (D,), jnp.float32), 0.1, 1.9),
        "final_gain": jnp.clip(1.0 + 0.18 * jax.random.normal(arg_keys[12], (D,), jnp.float32), 0.1, 1.9),
        "cross_query": draw_cross_query(jax.random.fold_in(arg_keys[17], 71), 0),
        "cross_key": draw_cross_key(jax.random.fold_in(arg_keys[17], 71), 0),
        "cross_value": centred(arg_keys[15], (D, HEADS * HEAD_DIM), D ** -0.5, 0.1875, ((1, 16),)),
        "cross_out": centred(arg_keys[16], (HEADS * HEAD_DIM, D), (8 * HEAD_DIM) ** -0.5, 0.1875, ((0, 16),)),
    }


EPSILON = 1e-06
MASKED = -1000000000.0

def row_scale(matrix):
    values = matrix.astype(jnp.float32)
    return lax.rsqrt(lax.optimization_barrier(jnp.mean(values * values, axis=1, keepdims=True)) + EPSILON)

def attend(queries, keys, values, allowed):
    heads = queries.shape[1] // HEAD_DIM

    def by_head(matrix):
        return jnp.transpose(matrix.reshape(matrix.shape[0], heads, HEAD_DIM), (1, 0, 2))

    def one_head(item):
        head_queries, head_keys, head_values = item
        scores = jnp.dot(head_queries, jnp.transpose(head_keys), preferred_element_type=jnp.float32) * HEAD_DIM ** (-0.5)
        scores = jnp.where(allowed, scores, MASKED)
        top = lax.optimization_barrier(jnp.max(scores, axis=1, keepdims=True))
        expo = jnp.exp(scores - top)
        total = lax.optimization_barrier(jnp.sum(expo, axis=1, keepdims=True))
        weights = expo.astype(jnp.bfloat16)
        return jnp.dot(weights, head_values, preferred_element_type=jnp.float32) / total
    context = lax.map(one_head, (by_head(queries), by_head(keys), by_head(values)))
    return jnp.transpose(context, (1, 0, 2)).reshape(queries.shape[0], heads * HEAD_DIM).astype(jnp.bfloat16)

def token_layout(block_protein, protein_length):
    count = block_protein.shape[0]
    order = jnp.arange(count, dtype=jnp.int32)
    same = block_protein[:, None] == block_protein[None, :]
    offset = lax.optimization_barrier(jnp.sum(same & (order[None, :] < order[:, None]), axis=1)).astype(jnp.int32)
    live = jnp.clip(protein_length[block_protein] - offset * BLOCK, 0, BLOCK)
    position = jnp.arange(BLOCK, dtype=jnp.int32)
    valid = (position[None, :] < live[:, None]).reshape(-1)
    owner = jnp.repeat(block_protein, BLOCK)
    return (owner, valid)

def reference(residues, block_protein, protein_length, decoder_group, enc_gain, enc_query, enc_key, enc_value, enc_out, decoder_states, query_protein, dec_gain, final_gain, cross_query, cross_key, cross_value, cross_out):
    owner, valid = token_layout(block_protein, protein_length)
    normed = (residues.astype(jnp.float32) * row_scale(residues) * enc_gain[None, :]).astype(jnp.bfloat16)
    enc_q = jnp.dot(normed, enc_query, preferred_element_type=jnp.float32).astype(jnp.bfloat16)
    enc_k = jnp.dot(normed, enc_key, preferred_element_type=jnp.float32).astype(jnp.bfloat16)
    enc_v = jnp.dot(normed, enc_value, preferred_element_type=jnp.float32).astype(jnp.bfloat16)
    allowed = (owner[:, None] == owner[None, :]) & valid[None, :]
    context = attend(enc_q, enc_k, enc_v, allowed)
    encoded = (residues.astype(jnp.float32) + jnp.dot(context, enc_out, preferred_element_type=jnp.float32)).astype(jnp.bfloat16)
    scaled = (encoded.astype(jnp.float32) * final_gain[None, :]).astype(jnp.bfloat16)
    key_scale = row_scale(encoded)
    cross_k = (jnp.dot(scaled, cross_key, preferred_element_type=jnp.float32) * key_scale).astype(jnp.bfloat16)
    cross_v = (jnp.dot(scaled, cross_value, preferred_element_type=jnp.float32) * key_scale).astype(jnp.bfloat16)
    dec_normed = (decoder_states.astype(jnp.float32) * row_scale(decoder_states) * dec_gain[None, :]).astype(jnp.bfloat16)
    cross_q = jnp.dot(dec_normed, cross_query, preferred_element_type=jnp.float32).astype(jnp.bfloat16)
    owner_group = decoder_group[owner]
    query_group = (jnp.arange(decoder_states.shape[0], dtype=jnp.int32) // Q_DEV).astype(jnp.int32)
    cross_allowed = (query_protein[:, None] == owner[None, :]) & valid[None, :] & (owner_group[None, :] == query_group[:, None])
    cross_context = attend(cross_q, cross_k, cross_v, cross_allowed)
    decoded = (decoder_states.astype(jnp.float32) + jnp.dot(cross_context, cross_out, preferred_element_type=jnp.float32)).astype(jnp.bfloat16)
    return (encoded, decoded)
```

```python
import jax
import jax.numpy as jnp
import numpy as np
from jax import lax
from jax.experimental import pallas as pl
from jax.experimental.pallas import tpu as pltpu
from jax.sharding import PartitionSpec as P

HEAD_DIM = 128
BLOCK = 128
EPSILON = 1e-06
MASKED = -1000000000.0
SCALE = HEAD_DIM ** (-0.5)
BF16 = jnp.bfloat16
F32 = jnp.float32
VMEM_LIMIT = 56 * 1024 * 1024

VMEM = pl.BlockSpec(memory_space=pltpu.VMEM)
SMEM = pl.BlockSpec(memory_space=pltpu.SMEM)
ANY = pl.BlockSpec(memory_space=pl.ANY)

XA, XB, YA, YB = 1, 3, 4, 12
ORDERS = (((XA, XB, YA, YB), (XB, XA, YB, YA)), ((YA, YB, XA, XB), (YB, YA, XB, XA)))


def rms_scaled(x, gain):
    scale = lax.rsqrt(jnp.mean(x * x, axis=1, keepdims=True) + EPSILON)
    return (x * scale * gain).astype(BF16)


def dot(a, b):
    return jnp.dot(a, b, preferred_element_type=F32)


def dot_t(a, b):
    return lax.dot_general(a, b, (((1,), (1,)), ((), ())), preferred_element_type=F32)


def block_facts(blocks, protein_ref, length_ref):
    ids = [protein_ref[b] for b in range(blocks)]
    live = []
    for b in range(blocks):
        offset = jnp.int32(0)
        for other in range(b):
            offset += jnp.where(ids[other] == ids[b], BLOCK, 0)
        live.append(jnp.clip(length_ref[ids[b]] - offset, 0, BLOCK))
    return ids, live


def encoder_kernel(
    protein_ref,
    length_ref,
    residue_ref,
    gain_ref,
    wq_hbm,
    wk_hbm,
    wv_hbm,
    wo_hbm,
    out_ref,
    wq,
    wk,
    wv,
    wo,
    normed,
    q,
    k,
    v,
    context,
    sems,
):
    copies = [
        pltpu.make_async_copy(src, dst, sems.at[i])
        for i, (src, dst) in enumerate(((wq_hbm, wq), (wk_hbm, wk), (wv_hbm, wv), (wo_hbm, wo)))
    ]
    for copy in copies:
        copy.start()
    rows, width = residue_ref.shape
    blocks = rows // BLOCK
    inner = q.shape[1]
    ids, live = block_facts(blocks, protein_ref, length_ref)
    gain = gain_ref[...]
    for b in range(blocks):
        span = slice(b * BLOCK, (b + 1) * BLOCK)
        normed[span, :] = rms_scaled(residue_ref[span, :].astype(F32), gain)
    for copy, weight, result in zip(copies[:3], (wq, wk, wv), (q, k, v)):
        copy.wait()

        @pl.loop(0, inner // 256)
        def _(n):
            cols = pl.ds(pl.multiple_of(n * 256, 256), 256)
            result[:, cols] = dot(normed[...], weight[:, cols]).astype(BF16)

    lane = lax.broadcasted_iota(jnp.int32, (1, BLOCK), 1)

    @pl.loop(0, inner // HEAD_DIM)
    def _(h):
        cols = pl.ds(pl.multiple_of(h * HEAD_DIM, HEAD_DIM), HEAD_DIM)
        for b in range(blocks):
            low, high = max(0, b - 1), min(blocks, b + 2)
            span = slice(b * BLOCK, (b + 1) * BLOCK)
            keys = slice(low * BLOCK, high * BLOCK)
            scores = dot_t(q[span, cols], k[keys, cols]) * SCALE
            seen = jnp.concatenate(
                [
                    jnp.broadcast_to(lane < jnp.where(ids[o] == ids[b], live[o], 0), (BLOCK, BLOCK))
                    for o in range(low, high)
                ],
                axis=1,
            )
            scores = jnp.where(seen, scores, MASKED)
            top = jnp.max(scores, axis=1, keepdims=True)
            expo = jnp.exp(scores - top)
            total = jnp.sum(expo, axis=1, keepdims=True)
            mixed = dot(expo.astype(BF16), v[keys, cols])
            context[span, cols] = (mixed / total).astype(BF16)

    copies[3].wait()

    @pl.loop(0, width // 256)
    def _(n):
        cols = pl.ds(pl.multiple_of(n * 256, 256), 256)
        out_ref[cols, :] = dot(context[...], wo[:, cols]).T.astype(BF16)


def encoder(protein, length, residues, gain, wq, wk, wv, wo):
    rows, width = residues.shape
    inner = wq.shape[1]
    return pl.pallas_call(
        encoder_kernel,
        out_shape=jax.ShapeDtypeStruct((width, rows), BF16),
        in_specs=[SMEM, SMEM, VMEM, VMEM, ANY, ANY, ANY, ANY],
        out_specs=VMEM,
        scratch_shapes=[pltpu.VMEM((width, inner), BF16)] * 3
        + [pltpu.VMEM((inner, width), BF16), pltpu.VMEM((rows, width), BF16)]
        + [pltpu.VMEM((rows, inner), BF16)] * 4
        + [pltpu.SemaphoreType.DMA((4,))],
        compiler_params=pltpu.CompilerParams(vmem_limit_bytes=VMEM_LIMIT),
        cost_estimate=pl.CostEstimate(
            flops=2 * rows * width * inner * 4, bytes_accessed=8 * width * inner, transcendentals=rows * rows * 8
        ),
        name="encoder",
    )(protein, length, residues, gain, wq, wk, wv, wo)


def query_kernel(
    state_ref, dec_gain_ref, final_gain_ref, id_row_ref, id_col_ref, wq_ref, wk_ref, out_ref, back_ref, id_ref
):
    rows = state_ref.shape[0]
    id_row = id_row_ref[...]
    id_col = id_col_ref[...]
    down = lax.broadcasted_iota(jnp.int32, (rows, rows), 0)
    along = lax.broadcasted_iota(jnp.int32, (rows, rows), 1)
    before = (id_col < id_row) | ((id_col == id_row) & (down < along))
    place_row = jnp.sum(before.astype(F32), axis=0, keepdims=True).astype(jnp.int32)
    before = (id_row < id_col) | ((id_row == id_col) & (along < down))
    place_col = jnp.sum(before.astype(F32), axis=1, keepdims=True).astype(jnp.int32)
    chosen = down == place_row
    back_ref[...] = (along == place_col).astype(F32).astype(BF16)
    id_ref[...] = jnp.sum(jnp.where(chosen, id_row.astype(F32), 0.0), axis=1, keepdims=True)
    normed = rms_scaled(state_ref[...].astype(F32), dec_gain_ref[...])
    normed = dot(chosen.astype(F32).astype(BF16), normed).astype(BF16)
    gain = final_gain_ref[...]
    for pair in range(wq_ref.shape[1] // 256):
        queries = dot(normed, wq_ref[:, pair * 256 : (pair + 1) * 256]).astype(BF16)
        for side in range(2):
            h = pair * 2 + side
            head = queries[:, side * HEAD_DIM : (side + 1) * HEAD_DIM]
            back = dot_t(head, wk_ref[:, h * HEAD_DIM : (h + 1) * HEAD_DIM])
            out_ref[h] = (back * gain).astype(BF16)


def query_side(states, dec_gain, final_gain, ids, wq, wk):
    rows, width = states.shape
    inner = wq.shape[1]
    heads = inner // HEAD_DIM
    return pl.pallas_call(
        query_kernel,
        out_shape=(
            jax.ShapeDtypeStruct((heads, rows, width), BF16),
            jax.ShapeDtypeStruct((rows, rows), BF16),
            jax.ShapeDtypeStruct((rows, 1), F32),
        ),
        in_specs=[VMEM] * 7,
        out_specs=(VMEM,) * 3,
        compiler_params=pltpu.CompilerParams(vmem_limit_bytes=VMEM_LIMIT),
        cost_estimate=pl.CostEstimate(
            flops=4 * rows * width * inner, bytes_accessed=4 * width * inner + 2 * heads * rows * width, transcendentals=0
        ),
        name="query_side",
    )(states, dec_gain, final_gain, ids.reshape(1, rows), ids.reshape(rows, 1), wq, wk)


def placing_kernel(protein_ref, length_ref, group_ref, arrived_ref, own_ref, encoded_ref, placed_ref):
    sources, features, rows = arrived_ref.shape
    blocks = rows // BLOCK
    groups = placed_ref.shape[0]
    slots = placed_ref.shape[2] // BLOCK
    total = own_ref[...].astype(F32)
    sums = arrived_ref[0].astype(F32)
    for s in range(1, sources):
        sums = sums + arrived_ref[s].astype(F32)
    encoded_ref[...] = (total + sums).astype(BF16)
    ids, live = block_facts(blocks, protein_ref, length_ref)
    dest = [group_ref[ids[b]] for b in range(blocks)]
    rank = []
    for b in range(blocks):
        count = jnp.int32(0)
        for other in range(b):
            count += jnp.where(dest[other] == dest[b], 1, 0)
        rank.append(count)
    lane = lax.broadcasted_iota(jnp.int32, (16, BLOCK), 1)
    for d in range(groups):
        for s in range(slots):
            block, name, limit = jnp.int32(0), jnp.int32(-1), jnp.int32(0)
            for b in range(blocks):
                here = (dest[b] == d) & (rank[b] == s)
                block = jnp.where(here, b, block)
                name = jnp.where(here, ids[b], name)
                limit = jnp.where(here, live[b], limit)
            cols = slice(s * BLOCK, (s + 1) * BLOCK)
            start = pl.multiple_of(block * BLOCK, BLOCK)
            placed_ref[d, 0:features, cols] = encoded_ref[:, pl.ds(start, BLOCK)]
            placed_ref[d, features : features + 16, cols] = (
                jnp.where(lane < limit, name, -1).astype(F32).astype(BF16)
            )


def placing(protein, length, group, arrived, own, groups):
    sources, features, rows = arrived.shape
    slots = rows // BLOCK // 2
    return pl.pallas_call(
        placing_kernel,
        out_shape=(
            jax.ShapeDtypeStruct((features, rows), BF16),
            jax.ShapeDtypeStruct((groups, features + 16, slots * BLOCK), BF16),
        ),
        in_specs=[SMEM, SMEM, SMEM, VMEM, VMEM],
        out_specs=(VMEM, VMEM),
        compiler_params=pltpu.CompilerParams(vmem_limit_bytes=VMEM_LIMIT),
        name="placing",
    )(protein, length, group, arrived, own)


ROW_TILE = 32


def cross_kernel(
    start_ref,
    origin_ref,
    query_ref,
    id_ref,
    key_id_ref,
    gain_ref,
    back_ref,
    low_hbm,
    high_hbm,
    wv_hbm,
    wo_hbm,
    out_ref,
    keys,
    key_scale,
    mixed,
    context,
    wv,
    wo,
    key_sem,
    weight_sems,
):
    heads, rows, width = query_ref.shape
    groups, _, span = keys.shape
    chunks, _, part, _ = low_hbm.shape
    weight_copies = [
        pltpu.make_async_copy(wv_hbm, wv, weight_sems.at[0]),
        pltpu.make_async_copy(wo_hbm, wo, weight_sems.at[1]),
    ]
    key_copies = []
    for half, source in enumerate((low_hbm, high_hbm)):
        for j in range(chunks):
            at = pl.multiple_of(origin_ref[half * chunks + j] * (2 * part) + half * part, part)
            key_copies.append(pltpu.make_async_copy(source.at[j], keys.at[:, pl.ds(at, part), :], key_sem))
    for copy in key_copies:
        copy.start()
    for copy in weight_copies:
        copy.start()
    for copy in key_copies:
        copy.wait()

    @pl.loop(0, groups)
    def _(e):
        squares = jnp.zeros((8, span), F32)
        for piece in range(width // 128):
            values = keys[e, piece * 128 : (piece + 1) * 128, :].astype(F32)
            squares = squares + jnp.sum((values * values).reshape(16, 8, span), axis=0)
        total = jnp.sum(squares, axis=0, keepdims=True)
        key_scale[e] = lax.rsqrt(total / width + EPSILON)

    gain = gain_ref[...]
    flat = heads * ROW_TILE

    @pl.loop(0, groups)
    def _(e):
        first = start_ref[e] // ROW_TILE
        last = (start_ref[e + 1] + ROW_TILE - 1) // ROW_TILE

        @pl.when(start_ref[e + 1] > start_ref[e])
        def _():
            @pl.loop(first, last)
            def _(i):
                at = pl.ds(pl.multiple_of(i * ROW_TILE, ROW_TILE), ROW_TILE)
                ids = id_ref[at, :]
                scale = key_scale[e]
                seen = ids == key_id_ref[e]
                mine = (ids >= (e * 4).astype(F32)) & (ids < (e * 4 + 4).astype(F32))
                scores = dot(query_ref[:, at, :].reshape(flat, width), keys[e]) * (scale * SCALE)
                scores = jnp.where(seen[None], scores.reshape(heads, ROW_TILE, span), MASKED)
                top = jnp.max(scores, axis=2, keepdims=True)
                expo = jnp.exp(scores - top)
                total = jnp.sum(expo, axis=2, keepdims=True)
                weights = (expo * scale[None]).astype(BF16).reshape(flat, span)
                spread = dot_t(weights, keys[e]).reshape(heads, ROW_TILE, width)
                spread = (spread * (1.0 / total) * gain[None]).astype(BF16)
                mixed[:, at, :] = jnp.where(mine[None], spread, mixed[:, at, :])

    for copy in weight_copies:
        copy.wait()

    @pl.loop(0, heads)
    def _(h):
        cols = pl.ds(pl.multiple_of(h * HEAD_DIM, HEAD_DIM), HEAD_DIM)
        context[:, cols] = dot(mixed[h], wv[:, cols]).astype(BF16)

    context[...] = dot(back_ref[...], context[...]).astype(BF16)

    @pl.loop(0, width // 256)
    def _(n):
        cols = pl.ds(pl.multiple_of(n * 256, 256), 256)
        out_ref[:, cols] = dot(context[...], wo[:, cols]).astype(BF16)


def cross(starts, origins, queries, ids, key_ids, gain, back, low, high, wv, wo):
    heads, rows, width = queries.shape
    groups, span = key_ids.shape[0], key_ids.shape[2]
    inner = wv.shape[1]
    return pl.pallas_call(
        cross_kernel,
        out_shape=jax.ShapeDtypeStruct((rows, width), BF16),
        in_specs=[SMEM, SMEM] + [VMEM] * 5 + [ANY] * 4,
        out_specs=VMEM,
        scratch_shapes=[
            pltpu.VMEM((groups, width, span), BF16),
            pltpu.VMEM((groups, 1, span), F32),
            pltpu.VMEM((heads, rows, width), BF16),
            pltpu.VMEM((rows, inner), BF16),
            pltpu.VMEM((width, inner), BF16),
            pltpu.VMEM((inner, width), BF16),
            pltpu.SemaphoreType.DMA,
            pltpu.SemaphoreType.DMA((2,)),
        ],
        compiler_params=pltpu.CompilerParams(vmem_limit_bytes=VMEM_LIMIT),
        cost_estimate=pl.CostEstimate(
            flops=8 * rows * width * inner, bytes_accessed=2 * groups * width * span, transcendentals=rows * span * heads
        ),
        name="cross",
    )(starts, origins, queries, ids, key_ids, gain, back, low, high, wv, wo)


def exchange(x, groups, tensor, half, step):
    pairs = [
        (d * tensor + t, d * tensor + (t ^ ORDERS[d % 2][half][step]))
        for d in range(groups)
        for t in range(tensor)
    ]
    return lax.ppermute(x, ("dp", "tensor"), pairs)


def gathered(low, high, groups, tensor):
    halves = [low[None], high[None]]
    for step in range(4):
        got = [exchange(halves[h], groups, tensor, h, step) for h in range(2)]
        halves = [jnp.concatenate([halves[h], got[h]], axis=0) for h in range(2)]
    return halves


def origin_masks():
    table = np.zeros((2, 2, 16), np.int32)
    for core in range(2):
        for half in range(2):
            for j in range(16):
                for step in range(4):
                    if j >> step & 1:
                        table[core, half, j] ^= ORDERS[core][half][step]
    return table.reshape(2, 32)


def body(
    residues,
    block_protein,
    protein_length,
    decoder_group,
    enc_gain,
    enc_query,
    enc_key,
    enc_value,
    enc_out,
    decoder_states,
    query_protein,
    dec_gain,
    final_gain,
    cross_query,
    cross_key,
    cross_value,
    cross_out,
):
    groups = lax.axis_size("dp")
    tensor = lax.axis_size("tensor")
    dp_index = lax.axis_index("dp")
    tensor_index = lax.axis_index("tensor")
    rows, width = residues.shape
    query_rows = decoder_states.shape[0]
    slice_width = width // tensor
    part = slice_width // 2

    partial_sums = encoder(
        block_protein, protein_length, residues, enc_gain.reshape(1, width), enc_query, enc_key, enc_value, enc_out
    )
    arrived = lax.all_to_all(
        partial_sums.reshape(tensor, slice_width, rows), "tensor", split_axis=0, concat_axis=0, tiled=True
    )
    queries, back, sorted_ids = query_side(
        decoder_states, dec_gain.reshape(1, width), final_gain.reshape(1, width), query_protein, cross_query, cross_key
    )
    bounds = 4 * jnp.arange(groups + 1, dtype=jnp.int32)
    starts = jnp.sum((query_protein[None, :] < bounds[:, None]).astype(jnp.int32), axis=1)
    masks = origin_masks()
    origins = tensor_index.astype(jnp.int32) ^ jnp.where(dp_index % 2 == 0, masks[0], masks[1])
    own = lax.dynamic_slice_in_dim(residues, tensor_index * slice_width, slice_width, 1).T
    encoded, placed = placing(block_protein, protein_length, decoder_group, arrived, own, groups)
    received = lax.all_to_all(placed, "dp", split_axis=0, concat_axis=0, tiled=True)
    low, high = gathered(received[:, :part], received[:, part : 2 * part], groups, tensor)
    key_ids = received[:, slice_width : slice_width + 1].astype(F32)
    outcome = cross(
        starts,
        origins,
        queries,
        sorted_ids,
        key_ids,
        final_gain.reshape(1, width),
        back,
        low,
        high,
        cross_value,
        cross_out,
    )
    share = query_rows // tensor
    mixed = lax.all_to_all(
        outcome.reshape(tensor, share, width), "tensor", split_axis=0, concat_axis=0, tiled=True
    )
    mixed = mixed.astype(F32).sum(axis=0)
    own_rows = lax.dynamic_slice_in_dim(decoder_states, tensor_index * share, share, 0)
    decoded = (own_rows.astype(F32) + mixed).astype(BF16)
    return (encoded.T, decoded)


def solution(mesh):
    in_specs = (
        P("dp", None),
        P("dp"),
        P(),
        P(),
        P(),
        P(None, "tensor"),
        P(None, "tensor"),
        P(None, "tensor"),
        P("tensor", None),
        P("dp", None),
        P("dp"),
        P(),
        P(),
        P(None, "tensor"),
        P(None, "tensor"),
        P(None, "tensor"),
        P("tensor", None),
    )
    out_specs = (P("dp", "tensor"), P(("dp", "tensor"), None))
    return jax.shard_map(body, mesh=mesh, in_specs=in_specs, out_specs=out_specs, check_vma=False)
```

```python
import jax
import jax.numpy as jnp
import numpy as np
from jax import lax
from jax.experimental import pallas as pl
from jax.experimental.pallas import tpu as pltpu
from jax.sharding import PartitionSpec as P

HEAD_DIM = 128
BLOCK = 128
EPSILON = 1e-06
MASKED = -1000000000.0
SCALE = HEAD_DIM ** (-0.5)
LOG2E = 1.4426950408889634
BF16 = jnp.bfloat16
F32 = jnp.float32
VMEM_LIMIT = 56 * 1024 * 1024

VMEM = pl.BlockSpec(memory_space=pltpu.VMEM)
SMEM = pl.BlockSpec(memory_space=pltpu.SMEM)
ANY = pl.BlockSpec(memory_space=pl.ANY)

XA, XB, YA, YB = 1, 3, 4, 12
ORDERS = (((XA, XB, YA, YB), (XB, XA, YB, YA)), ((YA, YB, XA, XB), (YB, YA, XB, XA)))


def rms_scaled(x, gain):
    scale = lax.rsqrt(jnp.mean(x * x, axis=1, keepdims=True) + EPSILON)
    return (x * scale * gain).astype(BF16)


def dot(a, b):
    return jnp.dot(a, b, preferred_element_type=F32)


def dot_t(a, b):
    return lax.dot_general(a, b, (((1,), (1,)), ((), ())), preferred_element_type=F32)


def block_facts(blocks, protein_ref, length_ref):
    ids = [protein_ref[b] for b in range(blocks)]
    live = []
    for b in range(blocks):
        offset = jnp.int32(0)
        for other in range(b):
            offset += jnp.where(ids[other] == ids[b], BLOCK, 0)
        live.append(jnp.clip(length_ref[ids[b]] - offset, 0, BLOCK))
    return ids, live


def encoder_kernel(
    protein_ref,
    length_ref,
    residue_ref,
    gain_ref,
    wq_hbm,
    wk_hbm,
    wv_hbm,
    wo_hbm,
    out_ref,
    wq,
    wk,
    wv,
    wo,
    normed,
    q,
    k,
    v,
    context,
    sems,
):
    copies = [
        pltpu.make_async_copy(src, dst, sems.at[i])
        for i, (src, dst) in enumerate(((wq_hbm, wq), (wk_hbm, wk), (wv_hbm, wv), (wo_hbm, wo)))
    ]
    for copy in copies:
        copy.start()
    rows, width = residue_ref.shape
    blocks = rows // BLOCK
    inner = q.shape[1]
    ids, live = block_facts(blocks, protein_ref, length_ref)
    gain = gain_ref[...]
    for b in range(blocks):
        span = slice(b * BLOCK, (b + 1) * BLOCK)
        normed[span, :] = rms_scaled(residue_ref[span, :].astype(F32), gain)
    for copy, weight, result in zip(copies[:3], (wq, wk, wv), (q, k, v)):
        copy.wait()

        result[...] = dot(normed[...], weight[...]).astype(BF16)

    lane = lax.broadcasted_iota(jnp.int32, (1, BLOCK), 1)
    mates, limits = [], []
    for b in range(blocks):
        mate, limit = jnp.int32(b), jnp.int32(0)
        for other in (b - 1, b + 1):
            if 0 <= other < blocks:
                same = ids[other] == ids[b]
                mate = jnp.where(same, other, mate)
                limit = jnp.where(same, live[other], limit)
        mates.append(mate)
        limits.append(limit)
    seen = [
        jnp.concatenate(
            [jnp.broadcast_to(lane < limit, (BLOCK, BLOCK)) for limit in (live[b], limits[b])], axis=1
        )
        for b in range(blocks)
    ]
    ones = jnp.ones((2 * BLOCK, HEAD_DIM), BF16)

    for h in range(inner // HEAD_DIM):
        cols = slice(h * HEAD_DIM, (h + 1) * HEAD_DIM)
        for b in range(blocks):
            span = slice(b * BLOCK, (b + 1) * BLOCK)
            mate = pl.ds(pl.multiple_of(mates[b] * BLOCK, BLOCK), BLOCK)
            window = jnp.concatenate([k[span, cols], k[mate, cols]], axis=0)
            scores = jnp.where(seen[b], dot_t(q[span, cols], window), MASKED)
            top = jnp.max(scores, axis=1, keepdims=True)
            weights = jnp.exp2((scores - top) * (SCALE * LOG2E)).astype(BF16)
            window = jnp.concatenate([v[span, cols], v[mate, cols]], axis=0)
            mixed = dot(weights, jnp.concatenate([window, ones], axis=1))
            context[span, cols] = (mixed[:, :HEAD_DIM] / mixed[:, HEAD_DIM:]).astype(BF16)

    copies[3].wait()

    out_ref[...] = dot(context[...], wo[...]).astype(BF16).T


def encoder(protein, length, residues, gain, wq, wk, wv, wo):
    rows, width = residues.shape
    inner = wq.shape[1]
    return pl.pallas_call(
        encoder_kernel,
        out_shape=jax.ShapeDtypeStruct((width, rows), BF16),
        in_specs=[SMEM, SMEM, VMEM, VMEM, ANY, ANY, ANY, ANY],
        out_specs=VMEM,
        scratch_shapes=[pltpu.VMEM((width, inner), BF16)] * 3
        + [pltpu.VMEM((inner, width), BF16), pltpu.VMEM((rows, width), BF16)]
        + [pltpu.VMEM((rows, inner), BF16)] * 4
        + [pltpu.SemaphoreType.DMA((4,))],
        compiler_params=pltpu.CompilerParams(vmem_limit_bytes=VMEM_LIMIT),
        cost_estimate=pl.CostEstimate(
            flops=2 * rows * width * inner * 4, bytes_accessed=8 * width * inner, transcendentals=rows * rows * 8
        ),
        name="encoder",
    )(protein, length, residues, gain, wq, wk, wv, wo)


def query_kernel(
    state_ref,
    dec_gain_ref,
    final_gain_ref,
    gain_col_ref,
    id_row_ref,
    id_col_ref,
    wq_ref,
    wk_ref,
    wv_ref,
    out_ref,
    back_ref,
    id_ref,
    gained_ref,
):
    rows = state_ref.shape[0]
    id_row = id_row_ref[...]
    id_col = id_col_ref[...]
    down = lax.broadcasted_iota(jnp.int32, (rows, rows), 0)
    along = lax.broadcasted_iota(jnp.int32, (rows, rows), 1)
    before = (id_col < id_row) | ((id_col == id_row) & (down < along))
    place_row = jnp.sum(before.astype(F32), axis=0, keepdims=True).astype(jnp.int32)
    before = (id_row < id_col) | ((id_row == id_col) & (along < down))
    place_col = jnp.sum(before.astype(F32), axis=1, keepdims=True).astype(jnp.int32)
    chosen = down == place_row
    back_ref[...] = (along == place_col).astype(F32).astype(BF16)
    id_ref[...] = jnp.sum(jnp.where(chosen, id_row.astype(F32), 0.0), axis=1, keepdims=True)
    normed = rms_scaled(state_ref[...].astype(F32), dec_gain_ref[...])
    normed = dot(chosen.astype(F32).astype(BF16), normed).astype(BF16)
    gained_ref[...] = (wv_ref[...].astype(F32) * gain_col_ref[...]).astype(BF16)
    gain = final_gain_ref[...]
    for pair in range(wq_ref.shape[1] // 256):
        queries = dot(normed, wq_ref[:, pair * 256 : (pair + 1) * 256]).astype(BF16)
        for side in range(2):
            h = pair * 2 + side
            head = queries[:, side * HEAD_DIM : (side + 1) * HEAD_DIM]
            back = dot_t(head, wk_ref[:, h * HEAD_DIM : (h + 1) * HEAD_DIM])
            out_ref[h] = (back * gain).astype(BF16)


def query_side(states, dec_gain, final_gain, ids, wq, wk, wv):
    rows, width = states.shape
    inner = wq.shape[1]
    heads = inner // HEAD_DIM
    return pl.pallas_call(
        query_kernel,
        out_shape=(
            jax.ShapeDtypeStruct((heads, rows, width), BF16),
            jax.ShapeDtypeStruct((rows, rows), BF16),
            jax.ShapeDtypeStruct((rows, 1), F32),
            jax.ShapeDtypeStruct((width, inner), BF16),
        ),
        in_specs=[VMEM] * 9,
        out_specs=(VMEM,) * 4,
        compiler_params=pltpu.CompilerParams(vmem_limit_bytes=VMEM_LIMIT),
        cost_estimate=pl.CostEstimate(
            flops=4 * rows * width * inner, bytes_accessed=4 * width * inner + 2 * heads * rows * width, transcendentals=0
        ),
        name="query_side",
    )(
        states,
        dec_gain.reshape(1, width),
        final_gain.reshape(1, width),
        final_gain.reshape(width, 1),
        ids.reshape(1, rows),
        ids.reshape(rows, 1),
        wq,
        wk,
        wv,
    )


def placing_kernel(protein_ref, length_ref, group_ref, arrived_ref, own_ref, encoded_ref, placed_ref):
    sources, features, rows = arrived_ref.shape
    blocks = rows // BLOCK
    groups = placed_ref.shape[0]
    slots = placed_ref.shape[2] // BLOCK
    total = own_ref[...].astype(F32)
    sums = arrived_ref[0].astype(F32)
    for s in range(1, sources):
        sums = sums + arrived_ref[s].astype(F32)
    encoded_ref[...] = (total + sums).astype(BF16)
    ids, live = block_facts(blocks, protein_ref, length_ref)
    dest = [group_ref[ids[b]] for b in range(blocks)]
    rank = []
    for b in range(blocks):
        count = jnp.int32(0)
        for other in range(b):
            count += jnp.where(dest[other] == dest[b], 1, 0)
        rank.append(count)
    lane = lax.broadcasted_iota(jnp.int32, (16, BLOCK), 1)
    for d in range(groups):
        for s in range(slots):
            block, name, limit = jnp.int32(0), jnp.int32(-1), jnp.int32(0)
            for b in range(blocks):
                here = (dest[b] == d) & (rank[b] == s)
                block = jnp.where(here, b, block)
                name = jnp.where(here, ids[b], name)
                limit = jnp.where(here, live[b], limit)
            cols = slice(s * BLOCK, (s + 1) * BLOCK)
            start = pl.multiple_of(block * BLOCK, BLOCK)
            placed_ref[d, 0:features, cols] = encoded_ref[:, pl.ds(start, BLOCK)]
            placed_ref[d, features : features + 16, cols] = (
                jnp.where(lane < limit, name, -1).astype(F32).astype(BF16)
            )


def placing(protein, length, group, arrived, own, groups):
    sources, features, rows = arrived.shape
    slots = rows // BLOCK // 2
    return pl.pallas_call(
        placing_kernel,
        out_shape=(
            jax.ShapeDtypeStruct((features, rows), BF16),
            jax.ShapeDtypeStruct((groups, features + 16, slots * BLOCK), BF16),
        ),
        in_specs=[SMEM, SMEM, SMEM, VMEM, VMEM],
        out_specs=(VMEM, VMEM),
        compiler_params=pltpu.CompilerParams(vmem_limit_bytes=VMEM_LIMIT),
        name="placing",
    )(protein, length, group, arrived, own)


ROW_TILE = 32
TOGETHER = 4


def cross_kernel(
    start_ref,
    origin_ref,
    query_ref,
    id_ref,
    key_id_ref,
    back_ref,
    low_ref,
    low_far_ref,
    high_ref,
    high_far_ref,
    wv_hbm,
    wo_hbm,
    out_ref,
    keys,
    key_scale,
    mixed,
    context,
    wv,
    wo,
    item_group,
    item_tile,
    key_sem,
    weight_sems,
):
    heads, rows, width = query_ref.shape
    groups, _, span = keys.shape
    chunks, _, part, _ = low_ref.shape
    weight_copies = [
        pltpu.make_async_copy(wv_hbm, wv, weight_sems.at[0]),
        pltpu.make_async_copy(wo_hbm, wo, weight_sems.at[1]),
    ]
    key_copies = []
    for piece, source in enumerate((low_ref, low_far_ref, high_ref, high_far_ref)):
        for j in range(chunks):
            at = pl.multiple_of(origin_ref[piece * chunks + j] * (2 * part) + piece // 2 * part, part)
            key_copies.append(pltpu.make_async_copy(source.at[j], keys.at[:, pl.ds(at, part), :], key_sem))
    for copy in key_copies:
        copy.start()
    for copy in weight_copies:
        copy.start()
    for copy in key_copies:
        copy.wait()

    @pl.loop(0, groups)
    def _(e):
        squares = jnp.zeros((8, span), F32)
        for piece in range(width // 128):
            values = keys[e, piece * 128 : (piece + 1) * 128, :].astype(F32)
            squares = squares + jnp.sum((values * values).reshape(16, 8, span), axis=0)
        total = jnp.sum(squares, axis=0, keepdims=True)
        key_scale[e] = lax.rsqrt(total / width + EPSILON)

    flat = heads * ROW_TILE

    def listed(e, count):
        first = start_ref[e] // ROW_TILE
        last = jnp.where(start_ref[e + 1] > start_ref[e], (start_ref[e + 1] + ROW_TILE - 1) // ROW_TILE, first)

        def note(i, at):
            item_group[at] = e
            item_tile[at] = i
            return at + 1

        return lax.fori_loop(first, last, note, count)

    items = lax.fori_loop(0, groups, listed, jnp.int32(0))
    for extra in range(TOGETHER - 1):
        item_group[items + extra] = item_group[items - 1]
        item_tile[items + extra] = item_tile[items - 1]

    @pl.loop(0, (items + TOGETHER - 1) // TOGETHER)
    def _(n):
        todo = [(item_group[n * TOGETHER + a], item_tile[n * TOGETHER + a]) for a in range(TOGETHER)]
        spots = [pl.ds(pl.multiple_of(i * ROW_TILE, ROW_TILE), ROW_TILE) for _, i in todo]
        scores = [
            dot(query_ref[:, at, :].reshape(flat, width), keys[e]) for (e, _), at in zip(todo, spots)
        ]
        weights = []
        for (e, _), at, raw in zip(todo, spots, scores):
            scale = key_scale[e]
            seen = id_ref[at, :] == key_id_ref[e]
            raw = (raw * (scale * (SCALE * LOG2E))).reshape(heads, ROW_TILE, span)
            raw = jnp.where(seen[None], raw, MASKED)
            expo = jnp.exp2(raw - jnp.max(raw, axis=2, keepdims=True))
            share = 1.0 / jnp.sum(expo, axis=2, keepdims=True)
            weights.append((expo * scale[None] * share).astype(BF16).reshape(flat, span))
        spreads = [dot_t(w, keys[e]) for w, (e, _) in zip(weights, todo)]
        for (e, _), at, spread in zip(todo, spots, spreads):
            ids = id_ref[at, :]
            mine = (ids >= (e * 4).astype(F32)) & (ids < (e * 4 + 4).astype(F32))
            spread = spread.astype(BF16).reshape(heads, ROW_TILE, width)
            mixed[:, at, :] = jnp.where(mine[None], spread, mixed[:, at, :])

    for copy in weight_copies:
        copy.wait()

    for h in range(heads):
        cols = slice(h * HEAD_DIM, (h + 1) * HEAD_DIM)
        context[:, cols] = dot(mixed[h], wv[:, cols]).astype(BF16)

    context[...] = dot(back_ref[...], context[...]).astype(BF16)

    out_ref[...] = dot(context[...], wo[...]).astype(BF16)


def cross(starts, origins, queries, ids, key_ids, back, pieces, wv, wo):
    heads, rows, width = queries.shape
    groups, span = key_ids.shape[0], key_ids.shape[2]
    inner = wv.shape[1]
    return pl.pallas_call(
        cross_kernel,
        out_shape=jax.ShapeDtypeStruct((rows, width), BF16),
        in_specs=[SMEM, SMEM] + [VMEM] * 8 + [ANY] * 2,
        out_specs=VMEM,
        scratch_shapes=[
            pltpu.VMEM((groups, width, span), BF16),
            pltpu.VMEM((groups, 1, span), F32),
            pltpu.VMEM((heads, rows, width), BF16),
            pltpu.VMEM((rows, inner), BF16),
            pltpu.VMEM((width, inner), BF16),
            pltpu.VMEM((inner, width), BF16),
            pltpu.SMEM((rows // ROW_TILE + groups + TOGETHER,), jnp.int32),
            pltpu.SMEM((rows // ROW_TILE + groups + TOGETHER,), jnp.int32),
            pltpu.SemaphoreType.DMA,
            pltpu.SemaphoreType.DMA((2,)),
        ],
        compiler_params=pltpu.CompilerParams(vmem_limit_bytes=VMEM_LIMIT),
        cost_estimate=pl.CostEstimate(
            flops=8 * rows * width * inner, bytes_accessed=2 * groups * width * span, transcendentals=rows * span * heads
        ),
        name="cross",
    )(starts, origins, queries, ids, key_ids, back, *pieces, wv, wo)


def exchange(x, groups, tensor, half, step):
    pairs = [
        (d * tensor + t, d * tensor + (t ^ ORDERS[d % 2][half][step]))
        for d in range(groups)
        for t in range(tensor)
    ]
    return lax.ppermute(x, ("dp", "tensor"), pairs)


def gathered(low, high, groups, tensor):
    halves = [low[None], high[None]]
    for step in range(3):
        got = [exchange(halves[h], groups, tensor, h, step) for h in range(2)]
        halves = [jnp.concatenate([halves[h], got[h]], axis=0) for h in range(2)]
    got = [exchange(halves[h], groups, tensor, h, 3) for h in range(2)]
    return halves[0], got[0], halves[1], got[1]


def origin_masks():
    table = np.zeros((2, 2, 16), np.int32)
    for core in range(2):
        for half in range(2):
            for j in range(16):
                for step in range(4):
                    if j >> step & 1:
                        table[core, half, j] ^= ORDERS[core][half][step]
    return table.reshape(2, 32)


def body(
    residues,
    block_protein,
    protein_length,
    decoder_group,
    enc_gain,
    enc_query,
    enc_key,
    enc_value,
    enc_out,
    decoder_states,
    query_protein,
    dec_gain,
    final_gain,
    cross_query,
    cross_key,
    cross_value,
    cross_out,
):
    groups = lax.axis_size("dp")
    tensor = lax.axis_size("tensor")
    dp_index = lax.axis_index("dp")
    tensor_index = lax.axis_index("tensor")
    rows, width = residues.shape
    query_rows = decoder_states.shape[0]
    slice_width = width // tensor
    part = slice_width // 2

    partial_sums = encoder(
        block_protein, protein_length, residues, enc_gain.reshape(1, width), enc_query, enc_key, enc_value, enc_out
    )
    arrived = lax.all_to_all(
        partial_sums.reshape(tensor, slice_width, rows), "tensor", split_axis=0, concat_axis=0, tiled=True
    )
    queries, back, sorted_ids, gained_value = query_side(
        decoder_states, dec_gain, final_gain, query_protein, cross_query, cross_key, cross_value
    )
    bounds = 4 * jnp.arange(groups + 1, dtype=jnp.int32)
    starts = jnp.sum((query_protein[None, :] < bounds[:, None]).astype(jnp.int32), axis=1)
    masks = origin_masks()
    origins = tensor_index.astype(jnp.int32) ^ jnp.where(dp_index % 2 == 0, masks[0], masks[1])
    own = lax.dynamic_slice_in_dim(residues, tensor_index * slice_width, slice_width, 1).T
    share = query_rows // tensor
    own_rows = lax.dynamic_slice_in_dim(decoder_states, tensor_index * share, share, 0).astype(F32)
    arrived, own, own_rows, queries, back, sorted_ids, gained_value, starts, origins = lax.optimization_barrier(
        (arrived, own, own_rows, queries, back, sorted_ids, gained_value, starts, origins)
    )
    encoded, placed = placing(block_protein, protein_length, decoder_group, arrived, own, groups)
    received = lax.all_to_all(placed, "dp", split_axis=0, concat_axis=0, tiled=True)
    pieces = gathered(received[:, :part], received[:, part : 2 * part], groups, tensor)
    key_ids = received[:, slice_width : slice_width + 1].astype(F32)
    outcome = cross(starts, origins, queries, sorted_ids, key_ids, back, pieces, gained_value, cross_out)
    mixed = lax.all_to_all(
        outcome.reshape(tensor, share, width), "tensor", split_axis=0, concat_axis=0, tiled=True
    )
    mixed = mixed.astype(F32).sum(axis=0)
    decoded = (own_rows + mixed).astype(BF16)
    return (encoded.T, decoded)


def solution(mesh):
    in_specs = (
        P("dp", None),
        P("dp"),
        P(),
        P(),
        P(),
        P(None, "tensor"),
        P(None, "tensor"),
        P(None, "tensor"),
        P("tensor", None),
        P("dp", None),
        P("dp"),
        P(),
        P(),
        P(None, "tensor"),
        P(None, "tensor"),
        P(None, "tensor"),
        P("tensor", None),
    )
    out_specs = (P("dp", "tensor"), P(("dp", "tensor"), None))
    return jax.shard_map(body, mesh=mesh, in_specs=in_specs, out_specs=out_specs, check_vma=False)
```

```python
import jax
import jax.numpy as jnp
import numpy as np
from jax import lax
from jax.experimental import pallas as pl
from jax.experimental.pallas import tpu as pltpu
from jax.sharding import PartitionSpec as P

HEAD_DIM = 128
BLOCK = 128
EPSILON = 1e-06
MASKED = -1000000000.0
SCALE = HEAD_DIM ** (-0.5)
LOG2E = 1.4426950408889634
BF16 = jnp.bfloat16
F32 = jnp.float32
MASKED_RAW = MASKED / SCALE
MASKED_LOG2 = MASKED * LOG2E
VMEM_LIMIT = 32 * 1024 * 1024
VMEM_ALL = 60 * 1024 * 1024

VMEM = pl.BlockSpec(memory_space=pltpu.VMEM)
SMEM = pl.BlockSpec(memory_space=pltpu.SMEM)
ANY = pl.BlockSpec(memory_space=pl.ANY)

XA, XB, YA, YB = 1, 3, 4, 12
ORDERS = (((XA, XB, YA, YB), (XB, XA, YB, YA)), ((YA, YB, XA, XB), (YB, YA, XB, XA)))


def rms_scaled(x, gain):
    scale = lax.rsqrt(jnp.mean(x * x, axis=1, keepdims=True) + EPSILON)
    return (x * scale * gain).astype(BF16)


def dot(a, b):
    return jnp.dot(a, b, preferred_element_type=F32)


def dot_t(a, b):
    return lax.dot_general(a, b, (((1,), (1,)), ((), ())), preferred_element_type=F32)


def block_facts(blocks, protein_ref, length_ref):
    ids = [protein_ref[b] for b in range(blocks)]
    live = []
    for b in range(blocks):
        offset = jnp.int32(0)
        for other in range(b):
            offset += jnp.where(ids[other] == ids[b], BLOCK, 0)
        live.append(jnp.clip(length_ref[ids[b]] - offset, 0, BLOCK))
    return ids, live


def encoder_kernel(
    protein_hbm,
    length_hbm,
    residue_hbm,
    gain_hbm,
    wq_hbm,
    wk_hbm,
    wv_hbm,
    wo_hbm,
    out_hbm,
    protein_ref,
    length_ref,
    residue_ref,
    gain_ref,
    out_ref,
    wq,
    wk,
    wv,
    wo,
    normed,
    q,
    k,
    v,
    context,
    sems,
):
    copies = [
        pltpu.make_async_copy(src, dst, sems.at[i])
        for i, (src, dst) in enumerate(
            (
                (gain_hbm, gain_ref),
                (residue_hbm, residue_ref),
                (wq_hbm, wq),
                (wk_hbm, wk),
                (wv_hbm, wv),
                (wo_hbm, wo),
                (protein_hbm, protein_ref),
                (length_hbm, length_ref),
            )
        )
    ]
    for copy in copies:
        copy.start()
    rows, width = residue_ref.shape
    blocks = rows // BLOCK
    inner = q.shape[1]
    copies[0].wait()
    copies[1].wait()
    gain = gain_ref[...]
    for b in range(blocks):
        span = slice(b * BLOCK, (b + 1) * BLOCK)
        normed[span, :] = rms_scaled(residue_ref[span, :].astype(F32), gain)
    for copy, weight, result in zip(copies[2:5], (wq, wk, wv), (q, k, v)):
        copy.wait()

        result[...] = dot(normed[...], weight[...]).astype(BF16)

    copies[6].wait()
    copies[7].wait()
    ids, live = block_facts(blocks, protein_ref, length_ref)
    lane = lax.broadcasted_iota(jnp.int32, (1, BLOCK), 1)
    mates, limits = [], []
    for b in range(blocks):
        mate, limit = jnp.int32(b), jnp.int32(0)
        for other in (b - 1, b + 1):
            if 0 <= other < blocks:
                same = ids[other] == ids[b]
                mate = jnp.where(same, other, mate)
                limit = jnp.where(same, live[other], limit)
        mates.append(mate)
        limits.append(limit)
    seen = [
        jnp.concatenate(
            [jnp.broadcast_to(lane < limit, (BLOCK, BLOCK)) for limit in (live[b], limits[b])], axis=1
        )
        for b in range(blocks)
    ]
    ones = jnp.ones((2 * BLOCK, HEAD_DIM), BF16)

    for h in range(inner // HEAD_DIM):
        cols = slice(h * HEAD_DIM, (h + 1) * HEAD_DIM)
        for b in range(blocks):
            span = slice(b * BLOCK, (b + 1) * BLOCK)
            mate = pl.ds(pl.multiple_of(mates[b] * BLOCK, BLOCK), BLOCK)
            window = jnp.concatenate([k[span, cols], k[mate, cols]], axis=0)
            scores = jnp.where(seen[b], dot_t(q[span, cols], window), MASKED_RAW)
            top = jnp.max(scores, axis=1, keepdims=True)
            weights = jnp.exp2((scores - top) * (SCALE * LOG2E)).astype(BF16)
            window = jnp.concatenate([v[span, cols], v[mate, cols]], axis=0)
            mixed = dot(weights, jnp.concatenate([window, ones], axis=1))
            context[span, cols] = (mixed[:, :HEAD_DIM] / mixed[:, HEAD_DIM:]).astype(BF16)

    copies[5].wait()
    half = width // 2
    stores = []
    for n in range(2):
        span = slice(n * half, (n + 1) * half)
        out_ref[span, :] = dot(context[...], wo[:, span]).astype(BF16).T
        stores.append(pltpu.make_async_copy(out_ref.at[span], out_hbm.at[span], sems.at[8 + n]))
        stores[n].start()
    for store in stores:
        store.wait()


def encoder(protein, length, residues, gain, wq, wk, wv, wo):
    rows, width = residues.shape
    inner = wq.shape[1]
    return pl.pallas_call(
        encoder_kernel,
        out_shape=jax.ShapeDtypeStruct((width, rows), BF16),
        in_specs=[ANY] * 8,
        out_specs=ANY,
        scratch_shapes=[
            pltpu.SMEM(protein.shape, jnp.int32),
            pltpu.SMEM(length.shape, jnp.int32),
            pltpu.VMEM((rows, width), BF16),
            pltpu.VMEM((1, width), F32),
            pltpu.VMEM((width, rows), BF16),
        ]
        + [pltpu.VMEM((width, inner), BF16)] * 3
        + [pltpu.VMEM((inner, width), BF16), pltpu.VMEM((rows, width), BF16)]
        + [pltpu.VMEM((rows, inner), BF16)] * 4
        + [pltpu.SemaphoreType.DMA((10,))],
        compiler_params=pltpu.CompilerParams(vmem_limit_bytes=VMEM_ALL),
        cost_estimate=pl.CostEstimate(
            flops=2 * rows * width * inner * 4, bytes_accessed=8 * width * inner, transcendentals=rows * rows * 8
        ),
        name="encoder",
    )(protein, length, residues, gain, wq, wk, wv, wo)


def as_column(row):
    size = row.shape[1]
    down = lax.broadcasted_iota(jnp.int32, (size, size), 0)
    along = lax.broadcasted_iota(jnp.int32, (size, size), 1)
    return jnp.sum(jnp.where(down == along, row, 0.0), axis=1, keepdims=True)


def query_kernel(
    protein_ref,
    length_ref,
    group_ref,
    where_ref,
    state_ref,
    dec_gain_ref,
    final_gain_ref,
    id_ref,
    wq_ref,
    wk_ref,
    wv_ref,
    residue_hbm,
    out_ref,
    back_ref,
    sorted_ref,
    gained_ref,
    own_ref,
    table_ref,
    start_ref,
    key_weight,
    columns,
    turned,
    sem,
):
    rows, width = state_ref.shape
    features = own_ref.shape[0]
    here, core = where_ref[0], where_ref[1]
    lanes = pl.ds(pl.multiple_of(here * features // BLOCK * BLOCK, BLOCK), BLOCK)
    copy = pltpu.make_async_copy(residue_hbm.at[:, lanes], columns, sem)
    copy.start()

    blocks = protein_ref.shape[0]
    slots = table_ref.shape[0] // 3
    each = slots // (start_ref.shape[0] - 1)
    ids, live = block_facts(blocks, protein_ref, length_ref)
    dest = [group_ref[ids[b]] for b in range(blocks)]
    for s in range(slots):
        table_ref[s] = 0
        table_ref[slots + s] = -1
        table_ref[2 * slots + s] = 0
    for b in range(blocks):
        rank = jnp.int32(0)
        for other in range(b):
            rank += jnp.where(dest[other] == dest[b], 1, 0)
        slot = dest[b] * each + rank
        table_ref[slot] = b
        table_ref[slots + slot] = ids[b]
        table_ref[2 * slots + slot] = live[b]

    id_row = id_ref[...].astype(F32)
    for e in range(start_ref.shape[0]):
        start_ref[e] = jnp.sum((id_row < 4.0 * e).astype(F32)).astype(jnp.int32)

    id_col = as_column(id_row)
    down = lax.broadcasted_iota(jnp.int32, (rows, rows), 0)
    along = lax.broadcasted_iota(jnp.int32, (rows, rows), 1)
    before = (id_col < id_row) | ((id_col == id_row) & (down < along))
    place_row = jnp.sum(before.astype(F32), axis=0, keepdims=True).astype(jnp.int32)
    before = (id_row < id_col) | ((id_row == id_col) & (along < down))
    place_col = jnp.sum(before.astype(F32), axis=1, keepdims=True).astype(jnp.int32)
    chosen = down == place_row
    back_ref[...] = (along == place_col).astype(F32).astype(BF16)
    sorted_ref[...] = jnp.sum(jnp.where(chosen, id_row, 0.0), axis=1, keepdims=True)
    normed = rms_scaled(state_ref[...].astype(F32), dec_gain_ref[...])
    normed = dot(chosen.astype(F32).astype(BF16), normed).astype(BF16)

    masks = origin_masks()
    part = features // 2
    gain_parts = [
        as_column(final_gain_ref[:, c * BLOCK : (c + 1) * BLOCK]) for c in range(width // BLOCK)
    ]
    gain_ref = turned
    for c, gain in enumerate(gain_parts):
        gain_ref[c * BLOCK : (c + 1) * BLOCK, :] = gain
    for index in range(width // part):
        origin = here ^ jnp.where(core == 0, int(masks[0, index]), int(masks[1, index]))
        rows_from = pl.ds(
            pl.multiple_of(origin * features + index // (width // features) * part, part), part
        )
        rows_to = slice(index * part, (index + 1) * part)
        gain = gain_ref[rows_from, :]
        key_weight[rows_to, :] = (wk_ref[rows_from, :].astype(F32) * gain).astype(BF16)
        gained_ref[rows_to, :] = (wv_ref[rows_from, :].astype(F32) * gain).astype(BF16)
    for pair in range(wq_ref.shape[1] // 256):
        queries = dot(normed, wq_ref[:, pair * 256 : (pair + 1) * 256]).astype(BF16)
        for side in range(2):
            h = pair * 2 + side
            head = queries[:, side * HEAD_DIM : (side + 1) * HEAD_DIM]
            out_ref[h] = dot_t(head, key_weight[:, h * HEAD_DIM : (h + 1) * HEAD_DIM]).astype(BF16)

    copy.wait()
    flipped = columns[...].astype(F32).T
    odd = here * features % BLOCK > 0
    own_ref[...] = jnp.where(odd, flipped[features:], flipped[:features])


def query_side(protein, length, group, where, states, dec_gain, final_gain, ids, wq, wk, wv, residues, groups):
    rows, width = states.shape
    inner = wq.shape[1]
    heads = inner // HEAD_DIM
    tokens = residues.shape[0]
    features = BLOCK // 2
    slots = groups * (tokens // BLOCK // 2)
    return pl.pallas_call(
        query_kernel,
        out_shape=(
            jax.ShapeDtypeStruct((heads, rows, width), BF16),
            jax.ShapeDtypeStruct((rows, rows), BF16),
            jax.ShapeDtypeStruct((rows, 1), F32),
            jax.ShapeDtypeStruct((width, inner), BF16),
            jax.ShapeDtypeStruct((features, tokens), F32),
            jax.ShapeDtypeStruct((3 * slots,), jnp.int32),
            jax.ShapeDtypeStruct((groups + 1,), jnp.int32),
        ),
        in_specs=[SMEM] * 4 + [VMEM] * 7 + [ANY],
        out_specs=(VMEM,) * 5 + (SMEM,) * 2,
        scratch_shapes=[
            pltpu.VMEM((width, inner), BF16),
            pltpu.VMEM((tokens, BLOCK), BF16),
            pltpu.VMEM((width, 1), F32),
            pltpu.SemaphoreType.DMA,
        ],
        compiler_params=pltpu.CompilerParams(vmem_limit_bytes=VMEM_LIMIT),
        cost_estimate=pl.CostEstimate(
            flops=4 * rows * width * inner, bytes_accessed=6 * width * inner + 2 * heads * rows * width, transcendentals=0
        ),
        name="query_side",
    )(
        protein,
        length,
        group,
        where,
        states,
        dec_gain.reshape(1, width),
        final_gain.reshape(1, width),
        ids.reshape(1, rows),
        wq,
        wk,
        wv,
        residues,
    )


def placing_kernel(table_hbm, arrived_hbm, own_hbm, encoded_ref, placed_ref, table_ref, own_ref, buffer, sems):
    sources, features, rows = buffer.shape
    groups = placed_ref.shape[0]
    each = placed_ref.shape[2] // BLOCK
    slots = groups * each
    copies = [
        pltpu.make_async_copy(arrived_hbm.at[s], buffer.at[s], sems.at[s]) for s in range(sources)
    ]
    table_copy = pltpu.make_async_copy(table_hbm, table_ref, sems.at[sources])
    own_copy = pltpu.make_async_copy(own_hbm, own_ref, sems.at[sources + 1])
    table_copy.start()
    own_copy.start()
    for copy in copies:
        copy.start()
    table_copy.wait()
    lane = lax.broadcasted_iota(jnp.int32, (16, BLOCK), 1)
    for d in range(groups):
        for s in range(each):
            slot = d * each + s
            placed_ref[d, features : features + 16, s * BLOCK : (s + 1) * BLOCK] = (
                jnp.where(lane < table_ref[2 * slots + slot], table_ref[slots + slot], -1).astype(F32).astype(BF16)
            )
    own_copy.wait()
    sums = own_ref[...]
    for s in range(sources):
        copies[s].wait()
        sums = sums + buffer[s].astype(F32)
    encoded_ref[...] = sums.astype(BF16)
    for d in range(groups):
        for s in range(each):
            start = pl.multiple_of(table_ref[d * each + s] * BLOCK, BLOCK)
            placed_ref[d, 0:features, s * BLOCK : (s + 1) * BLOCK] = encoded_ref[:, pl.ds(start, BLOCK)]


def placing(table, arrived, own, groups):
    sources, features, rows = arrived.shape
    each = table.shape[0] // 3 // groups
    return pl.pallas_call(
        placing_kernel,
        out_shape=(
            jax.ShapeDtypeStruct((features, rows), BF16),
            jax.ShapeDtypeStruct((groups, features + 16, each * BLOCK), BF16),
        ),
        in_specs=[ANY, ANY, ANY],
        out_specs=(VMEM, VMEM),
        scratch_shapes=[
            pltpu.SMEM(table.shape, jnp.int32),
            pltpu.VMEM(own.shape, F32),
            pltpu.VMEM(arrived.shape, BF16),
            pltpu.SemaphoreType.DMA((sources + 2,)),
        ],
        compiler_params=pltpu.CompilerParams(vmem_limit_bytes=VMEM_ALL),
        name="placing",
    )(table, arrived, own)


ROW_TILE = 32
TOGETHER = 4


def cross_kernel(
    start_hbm,
    query_ref,
    id_ref,
    key_id_ref,
    back_ref,
    low_ref,
    low_far_ref,
    high_ref,
    high_far_ref,
    wv_ref,
    wo_ref,
    out_hbm,
    out_ref,
    start_ref,
    key_scale,
    mixed,
    context,
    item_group,
    item_tile,
    sems,
):
    start_copy = pltpu.make_async_copy(start_hbm, start_ref, sems.at[0])
    start_copy.start()
    heads, rows, width = query_ref.shape
    chunks, groups, part, span = low_ref.shape
    pieces = (low_ref, low_far_ref, high_ref, high_far_ref)

    def keys(e):
        return jnp.concatenate([piece[:, e].reshape(chunks * part, span) for piece in pieces], axis=0)

    @pl.loop(0, groups)
    def _(e):
        squares = jnp.zeros((8, span), F32)
        for piece in pieces:
            for j in range(chunks):
                values = piece[j, e].astype(F32)
                squares = squares + jnp.sum((values * values).reshape(part // 8, 8, span), axis=0)
        total = jnp.sum(squares, axis=0, keepdims=True)
        key_scale[e] = lax.rsqrt(total / width + EPSILON)

    start_copy.wait()
    flat = heads * ROW_TILE

    def listed(e, count):
        first = start_ref[e] // ROW_TILE
        last = jnp.where(start_ref[e + 1] > start_ref[e], (start_ref[e + 1] + ROW_TILE - 1) // ROW_TILE, first)

        def note(i, at):
            item_group[at] = e
            item_tile[at] = i
            return at + 1

        return lax.fori_loop(first, last, note, count)

    items = lax.fori_loop(0, groups, listed, jnp.int32(0))
    for extra in range(TOGETHER - 1):
        item_group[items + extra] = item_group[items - 1]
        item_tile[items + extra] = item_tile[items - 1]

    @pl.loop(0, (items + TOGETHER - 1) // TOGETHER)
    def _(n):
        todo = [(item_group[n * TOGETHER + a], item_tile[n * TOGETHER + a]) for a in range(TOGETHER)]
        spots = [pl.ds(pl.multiple_of(i * ROW_TILE, ROW_TILE), ROW_TILE) for _, i in todo]
        scores = [
            dot(query_ref[:, at, :].reshape(flat, width), keys(e)) for (e, _), at in zip(todo, spots)
        ]
        weights = []
        for (e, _), at, raw in zip(todo, spots, scores):
            scale = key_scale[e]
            seen = id_ref[at, :] == key_id_ref[e]
            raw = (raw * (scale * (SCALE * LOG2E))).reshape(heads, ROW_TILE, span)
            raw = jnp.where(seen[None], raw, MASKED_LOG2)
            expo = jnp.exp2(raw - jnp.max(raw, axis=2, keepdims=True))
            share = 1.0 / jnp.sum(expo, axis=2, keepdims=True)
            weights.append((expo * scale[None] * share).astype(BF16).reshape(flat, span))
        spreads = [dot_t(w, keys(e)) for w, (e, _) in zip(weights, todo)]
        for (e, _), at, spread in zip(todo, spots, spreads):
            ids = id_ref[at, :]
            mine = (ids >= (e * 4).astype(F32)) & (ids < (e * 4 + 4).astype(F32))
            spread = spread.astype(BF16).reshape(heads, ROW_TILE, width)
            mixed[:, at, :] = jnp.where(mine[None], spread, mixed[:, at, :])

    for h in range(heads):
        cols = slice(h * HEAD_DIM, (h + 1) * HEAD_DIM)
        context[:, cols] = dot(mixed[h], wv_ref[:, cols]).astype(BF16)

    context[...] = dot(back_ref[...], context[...]).astype(BF16)

    half = rows // 2
    stores = []
    for n in range(2):
        span = slice(n * half, (n + 1) * half)
        out_ref[span, :] = dot(context[span, :], wo_ref[...]).astype(BF16)
        stores.append(pltpu.make_async_copy(out_ref.at[span], out_hbm.at[span], sems.at[1 + n]))
        stores[n].start()
    for store in stores:
        store.wait()


def cross(starts, queries, ids, key_ids, back, pieces, wv, wo):
    heads, rows, width = queries.shape
    groups, span = key_ids.shape[0], key_ids.shape[2]
    inner = wv.shape[1]
    items = rows // ROW_TILE + groups + TOGETHER
    return pl.pallas_call(
        cross_kernel,
        out_shape=jax.ShapeDtypeStruct((rows, width), BF16),
        in_specs=[ANY] + [VMEM] * 10,
        out_specs=ANY,
        scratch_shapes=[
            pltpu.VMEM((rows, width), BF16),
            pltpu.SMEM(starts.shape, jnp.int32),
            pltpu.VMEM((groups, 1, span), F32),
            pltpu.VMEM((heads, rows, width), BF16),
            pltpu.VMEM((rows, inner), BF16),
            pltpu.SMEM((items,), jnp.int32),
            pltpu.SMEM((items,), jnp.int32),
            pltpu.SemaphoreType.DMA((3,)),
        ],
        compiler_params=pltpu.CompilerParams(vmem_limit_bytes=VMEM_LIMIT),
        cost_estimate=pl.CostEstimate(
            flops=8 * rows * width * inner, bytes_accessed=2 * groups * width * span, transcendentals=rows * span * heads
        ),
        name="cross",
    )(starts, queries, ids, key_ids, back, *pieces, wv, wo)


def exchange(x, groups, tensor, half, step):
    pairs = [
        (d * tensor + t, d * tensor + (t ^ ORDERS[d % 2][half][step]))
        for d in range(groups)
        for t in range(tensor)
    ]
    return lax.ppermute(x, ("dp", "tensor"), pairs)


def gathered(low, high, groups, tensor):
    halves = [low[None], high[None]]
    for step in range(3):
        got = [exchange(halves[h], groups, tensor, h, step) for h in range(2)]
        halves = [jnp.concatenate([halves[h], got[h]], axis=0) for h in range(2)]
    got = [exchange(halves[h], groups, tensor, h, 3) for h in range(2)]
    return halves[0], got[0], halves[1], got[1]


def origin_masks():
    table = np.zeros((2, 2, 16), np.int32)
    for core in range(2):
        for half in range(2):
            for j in range(16):
                for step in range(4):
                    if j >> step & 1:
                        table[core, half, j] ^= ORDERS[core][half][step]
    return table.reshape(2, 32)


def body(
    residues,
    block_protein,
    protein_length,
    decoder_group,
    enc_gain,
    enc_query,
    enc_key,
    enc_value,
    enc_out,
    decoder_states,
    query_protein,
    dec_gain,
    final_gain,
    cross_query,
    cross_key,
    cross_value,
    cross_out,
):
    groups = lax.axis_size("dp")
    tensor = lax.axis_size("tensor")
    dp_index = lax.axis_index("dp")
    tensor_index = lax.axis_index("tensor")
    rows, width = residues.shape
    query_rows = decoder_states.shape[0]
    slice_width = width // tensor
    part = slice_width // 2

    partial_sums = encoder(
        block_protein, protein_length, residues, enc_gain.reshape(1, width), enc_query, enc_key, enc_value, enc_out
    )
    arrived = lax.all_to_all(
        partial_sums.reshape(tensor, slice_width, rows), "tensor", split_axis=0, concat_axis=0, tiled=True
    )
    where = jnp.stack([tensor_index, dp_index % 2]).astype(jnp.int32)
    queries, back, sorted_ids, gained_value, own, table, starts = query_side(
        block_protein,
        protein_length,
        decoder_group,
        where,
        decoder_states,
        dec_gain,
        final_gain,
        query_protein,
        cross_query,
        cross_key,
        cross_value,
        residues,
        groups,
    )
    share = query_rows // tensor
    own_rows = lax.dynamic_slice_in_dim(decoder_states, tensor_index * share, share, 0).astype(F32)
    arrived, own, queries = lax.optimization_barrier((arrived, own, queries))
    encoded, placed = placing(table, arrived, own, groups)
    received = lax.all_to_all(placed, "dp", split_axis=0, concat_axis=0, tiled=True)
    pieces = gathered(received[:, :part], received[:, part : 2 * part], groups, tensor)
    key_ids = received[:, slice_width : slice_width + 1].astype(F32)
    outcome = cross(starts, queries, sorted_ids, key_ids, back, pieces, gained_value, cross_out)
    mixed = lax.all_to_all(
        outcome.reshape(tensor, share, width), "tensor", split_axis=0, concat_axis=0, tiled=True
    )
    mixed, own_rows = lax.optimization_barrier((mixed, own_rows))
    mixed = mixed.astype(F32).sum(axis=0)
    decoded = (own_rows + mixed).astype(BF16)
    return (encoded.T, decoded)


def solution(mesh):
    in_specs = (
        P("dp", None),
        P("dp"),
        P(),
        P(),
        P(),
        P(None, "tensor"),
        P(None, "tensor"),
        P(None, "tensor"),
        P("tensor", None),
        P("dp", None),
        P("dp"),
        P(),
        P(),
        P(None, "tensor"),
        P(None, "tensor"),
        P(None, "tensor"),
        P("tensor", None),
    )
    out_specs = (P("dp", "tensor"), P(("dp", "tensor"), None))
    return jax.shard_map(body, mesh=mesh, in_specs=in_specs, out_specs=out_specs, check_vma=False)
```

```python
import jax
import jax.numpy as jnp
import numpy as np
from jax import lax
from jax.experimental import pallas as pl
from jax.experimental.pallas import tpu as pltpu
from jax.sharding import PartitionSpec as P

HEAD_DIM = 128
BLOCK = 128
EPSILON = 1e-06
MASKED = -1000000000.0
SCALE = HEAD_DIM ** (-0.5)
LOG2E = 1.4426950408889634
BF16 = jnp.bfloat16
F32 = jnp.float32
MASKED_RAW = MASKED / SCALE
MASKED_LOG2 = MASKED * LOG2E
VMEM_LIMIT = 32 * 1024 * 1024
VMEM_ALL = 60 * 1024 * 1024
VMEM_NEAR = 24 * 1024 * 1024
VMEM_PLACING = 8 * 1024 * 1024

VMEM = pl.BlockSpec(memory_space=pltpu.VMEM)
SMEM = pl.BlockSpec(memory_space=pltpu.SMEM)
ANY = pl.BlockSpec(memory_space=pl.ANY)

XA, XB, YA, YB = 1, 3, 4, 12
ORDERS = (((XA, XB, YA, YB), (XB, XA, YB, YA)), ((YA, YB, XA, XB), (YB, YA, XB, XA)))


def rms_scaled(x, gain):
    scale = lax.rsqrt(jnp.mean(x * x, axis=1, keepdims=True) + EPSILON)
    return (x * scale * gain).astype(BF16)


def dot(a, b):
    return jnp.dot(a, b, preferred_element_type=F32)


def dot_t(a, b):
    return lax.dot_general(a, b, (((1,), (1,)), ((), ())), preferred_element_type=F32)


def block_facts(blocks, protein_ref, length_ref):
    ids = [protein_ref[b] for b in range(blocks)]
    live = []
    for b in range(blocks):
        offset = jnp.int32(0)
        for other in range(b):
            offset += jnp.where(ids[other] == ids[b], BLOCK, 0)
        live.append(jnp.clip(length_ref[ids[b]] - offset, 0, BLOCK))
    return ids, live


def encoder_kernel(
    protein_hbm,
    length_hbm,
    residue_hbm,
    gain_hbm,
    wq_hbm,
    wk_hbm,
    wv_hbm,
    wo_hbm,
    out_hbm,
    protein_ref,
    length_ref,
    residue_ref,
    gain_ref,
    out_ref,
    wq,
    wk,
    wv,
    wo,
    normed,
    q,
    k,
    v,
    context,
    sems,
):
    copies = [
        pltpu.make_async_copy(src, dst, sems.at[i])
        for i, (src, dst) in enumerate(
            (
                (gain_hbm, gain_ref),
                (residue_hbm, residue_ref),
                (wq_hbm, wq),
                (wk_hbm, wk),
                (wv_hbm, wv),
                (wo_hbm, wo),
                (protein_hbm, protein_ref),
                (length_hbm, length_ref),
            )
        )
    ]
    for copy in copies:
        copy.start()
    rows, width = residue_ref.shape
    blocks = rows // BLOCK
    inner = q.shape[1]
    copies[0].wait()
    copies[1].wait()
    gain = gain_ref[...]
    for b in range(blocks):
        span = slice(b * BLOCK, (b + 1) * BLOCK)
        normed[span, :] = rms_scaled(residue_ref[span, :].astype(F32), gain)
    for copy, weight, result in zip(copies[2:5], (wq, wk, wv), (q, k, v)):
        copy.wait()

        result[...] = dot(normed[...], weight[...]).astype(BF16)

    copies[6].wait()
    copies[7].wait()
    ids, live = block_facts(blocks, protein_ref, length_ref)
    lane = lax.broadcasted_iota(jnp.int32, (1, BLOCK), 1)
    mates, limits = [], []
    for b in range(blocks):
        mate, limit = jnp.int32(b), jnp.int32(0)
        for other in (b - 1, b + 1):
            if 0 <= other < blocks:
                same = ids[other] == ids[b]
                mate = jnp.where(same, other, mate)
                limit = jnp.where(same, live[other], limit)
        mates.append(mate)
        limits.append(limit)
    seen = [
        jnp.concatenate(
            [jnp.broadcast_to(lane < limit, (BLOCK, BLOCK)) for limit in (live[b], limits[b])], axis=1
        )
        for b in range(blocks)
    ]
    ones = jnp.ones((2 * BLOCK, HEAD_DIM), BF16)

    for h in range(inner // HEAD_DIM):
        cols = slice(h * HEAD_DIM, (h + 1) * HEAD_DIM)
        for b in range(blocks):
            span = slice(b * BLOCK, (b + 1) * BLOCK)
            mate = pl.ds(pl.multiple_of(mates[b] * BLOCK, BLOCK), BLOCK)
            window = jnp.concatenate([k[span, cols], k[mate, cols]], axis=0)
            scores = jnp.where(seen[b], dot_t(q[span, cols], window), MASKED_RAW)
            top = jnp.max(scores, axis=1, keepdims=True)
            weights = jnp.exp2((scores - top) * (SCALE * LOG2E)).astype(BF16)
            window = jnp.concatenate([v[span, cols], v[mate, cols]], axis=0)
            mixed = dot(weights, jnp.concatenate([window, ones], axis=1))
            context[span, cols] = (mixed[:, :HEAD_DIM] / mixed[:, HEAD_DIM:]).astype(BF16)

    copies[5].wait()
    half = width // 2
    stores = []
    for n in range(2):
        span = slice(n * half, (n + 1) * half)
        out_ref[span, :] = dot(context[...], wo[:, span]).astype(BF16).T
        stores.append(pltpu.make_async_copy(out_ref.at[span], out_hbm.at[span], sems.at[8 + n]))
        stores[n].start()
    for store in stores:
        store.wait()


def encoder(protein, length, residues, gain, wq, wk, wv, wo):
    rows, width = residues.shape
    inner = wq.shape[1]
    return pl.pallas_call(
        encoder_kernel,
        out_shape=jax.ShapeDtypeStruct((width, rows), BF16),
        in_specs=[ANY] * 8,
        out_specs=ANY,
        scratch_shapes=[
            pltpu.SMEM(protein.shape, jnp.int32),
            pltpu.SMEM(length.shape, jnp.int32),
            pltpu.VMEM((rows, width), BF16),
            pltpu.VMEM((1, width), F32),
            pltpu.VMEM((width, rows), BF16),
        ]
        + [pltpu.VMEM((width, inner), BF16)] * 3
        + [pltpu.VMEM((inner, width), BF16), pltpu.VMEM((rows, width), BF16)]
        + [pltpu.VMEM((rows, inner), BF16)] * 4
        + [pltpu.SemaphoreType.DMA((10,))],
        compiler_params=pltpu.CompilerParams(vmem_limit_bytes=VMEM_ALL),
        cost_estimate=pl.CostEstimate(
            flops=2 * rows * width * inner * 4, bytes_accessed=8 * width * inner, transcendentals=rows * rows * 8
        ),
        name="encoder",
    )(protein, length, residues, gain, wq, wk, wv, wo)


def as_column(row):
    size = row.shape[1]
    down = lax.broadcasted_iota(jnp.int32, (size, size), 0)
    along = lax.broadcasted_iota(jnp.int32, (size, size), 1)
    return jnp.sum(jnp.where(down == along, row, 0.0), axis=1, keepdims=True)


def query_kernel(
    protein_ref,
    length_ref,
    group_ref,
    where_ref,
    state_ref,
    dec_gain_ref,
    final_gain_ref,
    id_ref,
    wq_ref,
    wk_ref,
    wv_ref,
    residue_hbm,
    out_ref,
    back_ref,
    sorted_ref,
    gained_ref,
    own_ref,
    key_id_ref,
    table_ref,
    start_ref,
    key_weight,
    columns,
    turned,
    sem,
):
    rows, width = state_ref.shape
    features = own_ref.shape[0]
    here, core = where_ref[0], where_ref[1]
    lanes = pl.ds(pl.multiple_of(here * features // BLOCK * BLOCK, BLOCK), BLOCK)
    copy = pltpu.make_async_copy(residue_hbm.at[:, lanes], columns, sem)
    copy.start()

    blocks = protein_ref.shape[0]
    slots = table_ref.shape[0]
    groups = key_id_ref.shape[0]
    each = slots // groups
    dest = [group_ref[protein_ref[b]] for b in range(blocks)]
    for s in range(slots):
        table_ref[s] = 0
    for b in range(blocks):
        rank = jnp.int32(0)
        for other in range(b):
            rank += jnp.where(dest[other] == dest[b], 1, 0)
        table_ref[dest[b] * each + rank] = b

    lane = lax.broadcasted_iota(jnp.int32, (1, BLOCK), 1)
    proteins = length_ref.shape[0] // groups
    for e in range(groups):
        taken = jnp.int32(0)
        names, limits = [jnp.int32(-1)] * each, [jnp.int32(0)] * each
        for p in range(e * proteins, (e + 1) * proteins):
            size = length_ref[p]
            count = lax.shift_right_logical(size + (BLOCK - 1), 7)
            wanted = group_ref[p] == where_ref[2]
            for s in range(each):
                offset = s - taken
                here_too = wanted & (offset >= 0) & (offset < count)
                names[s] = jnp.where(here_too, p, names[s])
                limits[s] = jnp.where(here_too, jnp.clip(size - offset * BLOCK, 0, BLOCK), limits[s])
            taken += jnp.where(wanted, count, 0)
        for s in range(each):
            key_id_ref[e, :, s * BLOCK : (s + 1) * BLOCK] = jnp.where(lane < limits[s], names[s], -1).astype(F32)

    id_row = id_ref[...].astype(F32)
    for e in range(start_ref.shape[0]):
        start_ref[e] = jnp.sum((id_row < 4.0 * e).astype(F32)).astype(jnp.int32)

    id_col = as_column(id_row)
    down = lax.broadcasted_iota(jnp.int32, (rows, rows), 0)
    along = lax.broadcasted_iota(jnp.int32, (rows, rows), 1)
    before = (id_col < id_row) | ((id_col == id_row) & (down < along))
    place_row = jnp.sum(before.astype(F32), axis=0, keepdims=True).astype(jnp.int32)
    before = (id_row < id_col) | ((id_row == id_col) & (along < down))
    place_col = jnp.sum(before.astype(F32), axis=1, keepdims=True).astype(jnp.int32)
    chosen = down == place_row
    back_ref[...] = (along == place_col).astype(F32).astype(BF16)
    sorted_ref[...] = jnp.sum(jnp.where(chosen, id_row, 0.0), axis=1, keepdims=True)
    normed = rms_scaled(state_ref[...].astype(F32), dec_gain_ref[...])
    normed = dot(chosen.astype(F32).astype(BF16), normed).astype(BF16)

    masks = origin_masks()
    part = features // 2
    gain_parts = [
        as_column(final_gain_ref[:, c * BLOCK : (c + 1) * BLOCK]) for c in range(width // BLOCK)
    ]
    gain_ref = turned
    for c, gain in enumerate(gain_parts):
        gain_ref[c * BLOCK : (c + 1) * BLOCK, :] = gain
    for index in range(width // part):
        origin = here ^ jnp.where(core == 0, int(masks[0, index]), int(masks[1, index]))
        rows_from = pl.ds(
            pl.multiple_of(origin * features + index // (width // features) * part, part), part
        )
        half, chunk = divmod(index, width // features)
        far, chunk = divmod(chunk, width // features // 2)
        place = (far * 2 + half) * (width // features // 2) + chunk
        rows_to = slice(place * part, (place + 1) * part)
        gain = gain_ref[rows_from, :]
        key_weight[rows_to, :] = (wk_ref[rows_from, :].astype(F32) * gain).astype(BF16)
        gained_ref[rows_to, :] = (wv_ref[rows_from, :].astype(F32) * gain).astype(BF16)
    for pair in range(wq_ref.shape[1] // 256):
        queries = dot(normed, wq_ref[:, pair * 256 : (pair + 1) * 256]).astype(BF16)
        for side in range(2):
            h = pair * 2 + side
            head = queries[:, side * HEAD_DIM : (side + 1) * HEAD_DIM]
            out_ref[h] = dot_t(head, key_weight[:, h * HEAD_DIM : (h + 1) * HEAD_DIM]).astype(BF16)

    copy.wait()
    flipped = columns[...].astype(F32).T
    odd = here * features % BLOCK > 0
    own_ref[...] = jnp.where(odd, flipped[features:], flipped[:features])


def query_side(protein, length, group, where, states, dec_gain, final_gain, ids, wq, wk, wv, residues, groups):
    rows, width = states.shape
    inner = wq.shape[1]
    heads = inner // HEAD_DIM
    tokens = residues.shape[0]
    features = BLOCK // 2
    slots = groups * (tokens // BLOCK // 2)
    return pl.pallas_call(
        query_kernel,
        out_shape=(
            jax.ShapeDtypeStruct((heads, rows, width), BF16),
            jax.ShapeDtypeStruct((rows, rows), BF16),
            jax.ShapeDtypeStruct((rows, 1), F32),
            jax.ShapeDtypeStruct((width, inner), BF16),
            jax.ShapeDtypeStruct((features, tokens), F32),
            jax.ShapeDtypeStruct((groups, 1, slots // groups * BLOCK), F32),
            jax.ShapeDtypeStruct((slots,), jnp.int32),
            jax.ShapeDtypeStruct((groups + 1,), jnp.int32),
        ),
        in_specs=[SMEM] * 4 + [VMEM] * 7 + [ANY],
        out_specs=(VMEM,) * 6 + (SMEM,) * 2,
        scratch_shapes=[
            pltpu.VMEM((width, inner), BF16),
            pltpu.VMEM((tokens, BLOCK), BF16),
            pltpu.VMEM((width, 1), F32),
            pltpu.SemaphoreType.DMA,
        ],
        compiler_params=pltpu.CompilerParams(vmem_limit_bytes=VMEM_LIMIT),
        cost_estimate=pl.CostEstimate(
            flops=4 * rows * width * inner, bytes_accessed=6 * width * inner + 2 * heads * rows * width, transcendentals=0
        ),
        name="query_side",
    )(
        protein,
        length,
        group,
        where,
        states,
        dec_gain.reshape(1, width),
        final_gain.reshape(1, width),
        ids.reshape(1, rows),
        wq,
        wk,
        wv,
        residues,
    )


def placing_kernel(table_ref, arrived_ref, own_ref, encoded_ref, placed_ref):
    groups = placed_ref.shape[0]
    each = placed_ref.shape[2] // BLOCK
    sums = own_ref[...]
    for s in range(arrived_ref.shape[0]):
        sums = sums + arrived_ref[s].astype(F32)
    encoded_ref[...] = sums.astype(BF16)
    for d in range(groups):
        for s in range(each):
            start = pl.multiple_of(table_ref[d * each + s] * BLOCK, BLOCK)
            placed_ref[d, :, s * BLOCK : (s + 1) * BLOCK] = encoded_ref[:, pl.ds(start, BLOCK)]


def placing(table, arrived, own, groups):
    _, features, rows = arrived.shape
    each = table.shape[0] // groups
    return pl.pallas_call(
        placing_kernel,
        out_shape=(
            jax.ShapeDtypeStruct((features, rows), BF16),
            jax.ShapeDtypeStruct((groups, features, each * BLOCK), BF16),
        ),
        in_specs=[SMEM, VMEM, VMEM],
        out_specs=(VMEM, VMEM),
        compiler_params=pltpu.CompilerParams(vmem_limit_bytes=VMEM_PLACING),
        name="placing",
    )(table, arrived, own)


ROW_TILE = 32
TOGETHER = 4


def stacked(pieces, e):
    chunks, _, part, span = pieces[0].shape
    return jnp.concatenate([piece[:, e].reshape(chunks * part, span) for piece in pieces], axis=0)


def square_sums(pieces, e):
    chunks, _, part, span = pieces[0].shape
    squares = jnp.zeros((8, span), F32)
    for piece in pieces:
        for j in range(chunks):
            values = piece[j, e].astype(F32)
            squares = squares + jnp.sum((values * values).reshape(part // 8, 8, span), axis=0)
    return squares


def tile_spot(i):
    return pl.ds(pl.multiple_of(i * ROW_TILE, ROW_TILE), ROW_TILE)


def near_kernel(start_ref, query_ref, low_ref, high_ref, score_ref, square_ref, work_ref):
    heads, rows, _ = query_ref.shape
    groups = low_ref.shape[1]
    near = 2 * low_ref.shape[0] * low_ref.shape[2]
    flat = heads * ROW_TILE
    room = (work_ref.shape[0] - 1) // 2
    pieces = (low_ref, high_ref)

    def listed(e, count):
        first = start_ref[e] // ROW_TILE
        last = jnp.where(start_ref[e + 1] > start_ref[e], (start_ref[e + 1] + ROW_TILE - 1) // ROW_TILE, first)

        def note(i, at):
            work_ref[at] = e
            work_ref[room + at] = i
            return at + 1

        return lax.fori_loop(first, last, note, count)

    items = lax.fori_loop(0, groups, listed, jnp.int32(0))
    for extra in range(TOGETHER - 1):
        work_ref[items + extra] = work_ref[items - 1]
        work_ref[room + items + extra] = work_ref[room + items - 1]
    work_ref[2 * room] = (items + TOGETHER - 1) // TOGETHER

    @pl.loop(0, groups)
    def _(e):
        square_ref[e] = square_sums(pieces, e)

    @pl.loop(0, work_ref[2 * room])
    def _(n):
        for a in range(TOGETHER):
            e, i = work_ref[n * TOGETHER + a], work_ref[room + n * TOGETHER + a]
            query = query_ref[:, tile_spot(i), 0:near].reshape(flat, near)
            score_ref[n * TOGETHER + a] = dot(query, stacked(pieces, e))


def work_room(rows, groups):
    return rows // ROW_TILE + groups + TOGETHER


def near_scores(starts, queries, low, high):
    heads, rows, width = queries.shape
    groups, span = low.shape[1], low.shape[3]
    flat = heads * ROW_TILE
    most = rows // ROW_TILE + groups - 1
    most = -(-most // TOGETHER) * TOGETHER
    return pl.pallas_call(
        near_kernel,
        out_shape=(
            jax.ShapeDtypeStruct((most, flat, span), F32),
            jax.ShapeDtypeStruct((groups, 8, span), F32),
            jax.ShapeDtypeStruct((2 * work_room(rows, groups) + 1,), jnp.int32),
        ),
        in_specs=[SMEM] + [VMEM] * 3,
        out_specs=(VMEM, VMEM, SMEM),
        compiler_params=pltpu.CompilerParams(vmem_limit_bytes=VMEM_NEAR),
        cost_estimate=pl.CostEstimate(
            flops=most * flat * span * width, bytes_accessed=4 * most * flat * span, transcendentals=0
        ),
        name="near_scores",
    )(starts, queries, low, high)


def cross_kernel(
    work_hbm,
    query_ref,
    score_ref,
    square_ref,
    id_ref,
    key_id_ref,
    back_ref,
    low_ref,
    high_ref,
    low_far_ref,
    high_far_ref,
    wv_ref,
    wo_ref,
    out_hbm,
    out_ref,
    work_ref,
    key_scale,
    mixed,
    context,
    sems,
):
    work_copy = pltpu.make_async_copy(work_hbm, work_ref, sems.at[0])
    work_copy.start()
    heads, rows, width = query_ref.shape
    chunks, groups, part, span = low_ref.shape
    near = 2 * chunks * part
    room = (work_ref.shape[0] - 1) // 2
    pieces = (low_ref, high_ref, low_far_ref, high_far_ref)

    @pl.loop(0, groups)
    def _(e):
        squares = square_ref[e] + square_sums(pieces[2:], e)
        total = jnp.sum(squares, axis=0, keepdims=True)
        key_scale[e] = lax.rsqrt(total / width + EPSILON)

    work_copy.wait()
    flat = heads * ROW_TILE

    @pl.loop(0, work_ref[2 * room])
    def _(n):
        numbers = [n * TOGETHER + a for a in range(TOGETHER)]
        todo = [(work_ref[at], work_ref[room + at]) for at in numbers]
        spots = [tile_spot(i) for _, i in todo]
        scores = [
            dot(query_ref[:, at, near:].reshape(flat, width - near), stacked(pieces[2:], e)) + score_ref[number]
            for (e, _), at, number in zip(todo, spots, numbers)
        ]
        weights = []
        for (e, _), at, raw in zip(todo, spots, scores):
            scale = key_scale[e]
            seen = id_ref[at, :] == key_id_ref[e]
            raw = (raw * (scale * (SCALE * LOG2E))).reshape(heads, ROW_TILE, span)
            raw = jnp.where(seen[None], raw, MASKED_LOG2)
            expo = jnp.exp2(raw - jnp.max(raw, axis=2, keepdims=True))
            share = 1.0 / jnp.sum(expo, axis=2, keepdims=True)
            weights.append((expo * scale[None] * share).astype(BF16).reshape(flat, span))
        spreads = [dot_t(w, stacked(pieces, e)) for w, (e, _) in zip(weights, todo)]
        for (e, _), at, spread in zip(todo, spots, spreads):
            ids = id_ref[at, :]
            mine = (ids >= (e * 4).astype(F32)) & (ids < (e * 4 + 4).astype(F32))
            spread = spread.astype(BF16).reshape(heads, ROW_TILE, width)
            mixed[:, at, :] = jnp.where(mine[None], spread, mixed[:, at, :])

    for h in range(heads):
        cols = slice(h * HEAD_DIM, (h + 1) * HEAD_DIM)
        context[:, cols] = dot(mixed[h], wv_ref[:, cols]).astype(BF16)

    context[...] = dot(back_ref[...], context[...]).astype(BF16)

    half = rows // 2
    stores = []
    for n in range(2):
        span = slice(n * half, (n + 1) * half)
        out_ref[span, :] = dot(context[span, :], wo_ref[...]).astype(BF16)
        stores.append(pltpu.make_async_copy(out_ref.at[span], out_hbm.at[span], sems.at[1 + n]))
        stores[n].start()
    for store in stores:
        store.wait()


def cross(work, queries, scores, squares, ids, key_ids, back, pieces, wv, wo):
    heads, rows, width = queries.shape
    groups, span = key_ids.shape[0], key_ids.shape[2]
    inner = wv.shape[1]
    return pl.pallas_call(
        cross_kernel,
        out_shape=jax.ShapeDtypeStruct((rows, width), BF16),
        in_specs=[ANY] + [VMEM] * 12,
        out_specs=ANY,
        scratch_shapes=[
            pltpu.VMEM((rows, width), BF16),
            pltpu.SMEM(work.shape, jnp.int32),
            pltpu.VMEM((groups, 1, span), F32),
            pltpu.VMEM((heads, rows, width), BF16),
            pltpu.VMEM((rows, inner), BF16),
            pltpu.SemaphoreType.DMA((3,)),
        ],
        compiler_params=pltpu.CompilerParams(vmem_limit_bytes=VMEM_LIMIT),
        cost_estimate=pl.CostEstimate(
            flops=8 * rows * width * inner, bytes_accessed=2 * groups * width * span, transcendentals=rows * span * heads
        ),
        name="cross",
    )(work, queries, scores, squares, ids, key_ids, back, *pieces, wv, wo)


def exchange(x, groups, tensor, half, step):
    pairs = [
        (d * tensor + t, d * tensor + (t ^ ORDERS[d % 2][half][step]))
        for d in range(groups)
        for t in range(tensor)
    ]
    return lax.ppermute(x, ("dp", "tensor"), pairs)


def gathered(low, high, groups, tensor):
    halves = [low[None], high[None]]
    for step in range(3):
        got = [exchange(halves[h], groups, tensor, h, step) for h in range(2)]
        halves = [jnp.concatenate([halves[h], got[h]], axis=0) for h in range(2)]
    got = [exchange(halves[h], groups, tensor, h, 3) for h in range(2)]
    return halves, got


def origin_masks():
    table = np.zeros((2, 2, 16), np.int32)
    for core in range(2):
        for half in range(2):
            for j in range(16):
                for step in range(4):
                    if j >> step & 1:
                        table[core, half, j] ^= ORDERS[core][half][step]
    return table.reshape(2, 32)


def body(
    residues,
    block_protein,
    protein_length,
    decoder_group,
    enc_gain,
    enc_query,
    enc_key,
    enc_value,
    enc_out,
    decoder_states,
    query_protein,
    dec_gain,
    final_gain,
    cross_query,
    cross_key,
    cross_value,
    cross_out,
):
    groups = lax.axis_size("dp")
    tensor = lax.axis_size("tensor")
    dp_index = lax.axis_index("dp")
    tensor_index = lax.axis_index("tensor")
    rows, width = residues.shape
    query_rows = decoder_states.shape[0]
    slice_width = width // tensor
    part = slice_width // 2

    partial_sums = encoder(
        block_protein, protein_length, residues, enc_gain.reshape(1, width), enc_query, enc_key, enc_value, enc_out
    )
    arrived = lax.all_to_all(
        partial_sums.reshape(tensor, slice_width, rows), "tensor", split_axis=0, concat_axis=0, tiled=True
    )
    where = jnp.stack([tensor_index, dp_index % 2, dp_index]).astype(jnp.int32)
    queries, back, sorted_ids, gained_value, own, key_ids, table, starts = query_side(
        block_protein,
        protein_length,
        decoder_group,
        where,
        decoder_states,
        dec_gain,
        final_gain,
        query_protein,
        cross_query,
        cross_key,
        cross_value,
        residues,
        groups,
    )
    share = query_rows // tensor
    own_rows = lax.dynamic_slice_in_dim(decoder_states, tensor_index * share, share, 0).astype(F32)
    arrived, own, queries = lax.optimization_barrier((arrived, own, queries))
    encoded, placed = placing(table, arrived, own, groups)
    received = lax.all_to_all(placed, "dp", split_axis=0, concat_axis=0, tiled=True)
    near, far = gathered(received[:, :part], received[:, part:], groups, tensor)
    scores, squares, work = near_scores(starts, queries, *near)
    outcome = cross(
        work, queries, scores, squares, sorted_ids, key_ids, back, (*near, *far), gained_value, cross_out
    )
    mixed = lax.all_to_all(
        outcome.reshape(tensor, share, width), "tensor", split_axis=0, concat_axis=0, tiled=True
    )
    mixed, own_rows = lax.optimization_barrier((mixed, own_rows))
    mixed = mixed.astype(F32).sum(axis=0)
    decoded = (own_rows + mixed).astype(BF16)
    return (encoded.T, decoded)


def solution(mesh):
    in_specs = (
        P("dp", None),
        P("dp"),
        P(),
        P(),
        P(),
        P(None, "tensor"),
        P(None, "tensor"),
        P(None, "tensor"),
        P("tensor", None),
        P("dp", None),
        P("dp"),
        P(),
        P(),
        P(None, "tensor"),
        P(None, "tensor"),
        P(None, "tensor"),
        P("tensor", None),
    )
    out_specs = (P("dp", "tensor"), P(("dp", "tensor"), None))
    return jax.shard_map(body, mesh=mesh, in_specs=in_specs, out_specs=out_specs, check_vma=False)
```

```python
import jax
import jax.numpy as jnp
import numpy as np
from jax import lax
from jax.experimental import pallas as pl
from jax.experimental.pallas import tpu as pltpu
from jax.sharding import PartitionSpec as P

HEAD_DIM = 128
BLOCK = 128
EPSILON = 1e-06
MASKED = -1000000000.0
SCALE = HEAD_DIM ** (-0.5)
LOG2E = 1.4426950408889634
BF16 = jnp.bfloat16
F32 = jnp.float32
MASKED_RAW = MASKED / SCALE
MASKED_LOG2 = MASKED * LOG2E
VMEM_LIMIT = 32 * 1024 * 1024
VMEM_ALL = 60 * 1024 * 1024
VMEM_NEAR = 24 * 1024 * 1024
VMEM_PLACING = 8 * 1024 * 1024

VMEM = pl.BlockSpec(memory_space=pltpu.VMEM)
SMEM = pl.BlockSpec(memory_space=pltpu.SMEM)
ANY = pl.BlockSpec(memory_space=pl.ANY)

XA, XB, YA, YB = 1, 3, 4, 12
ORDERS = ((XA, XB, YA, YB), (XB, XA, YB, YA), (YA, YB, XA, XB), (YB, YA, XB, XA))
CHAINS = len(ORDERS)


def rms_scaled(x, gain):
    scale = lax.rsqrt(jnp.mean(x * x, axis=1, keepdims=True) + EPSILON)
    return (x * scale * gain).astype(BF16)


def dot(a, b):
    return jnp.dot(a, b, preferred_element_type=F32)


def dot_t(a, b):
    return lax.dot_general(a, b, (((1,), (1,)), ((), ())), preferred_element_type=F32)


def block_facts(blocks, protein_ref, length_ref):
    ids = [protein_ref[b] for b in range(blocks)]
    live = []
    for b in range(blocks):
        offset = jnp.int32(0)
        for other in range(b):
            offset += jnp.where(ids[other] == ids[b], BLOCK, 0)
        live.append(jnp.clip(length_ref[ids[b]] - offset, 0, BLOCK))
    return ids, live


def encoder_kernel(
    protein_hbm,
    length_hbm,
    residue_hbm,
    gain_hbm,
    wq_hbm,
    wk_hbm,
    wv_hbm,
    wo_hbm,
    out_hbm,
    protein_ref,
    length_ref,
    residue_ref,
    gain_ref,
    out_ref,
    wq,
    wk,
    wv,
    wo,
    normed,
    q,
    k,
    v,
    context,
    sems,
):
    copies = [
        pltpu.make_async_copy(src, dst, sems.at[i])
        for i, (src, dst) in enumerate(
            (
                (gain_hbm, gain_ref),
                (residue_hbm, residue_ref),
                (wq_hbm, wq),
                (wk_hbm, wk),
                (wv_hbm, wv),
                (wo_hbm, wo),
                (protein_hbm, protein_ref),
                (length_hbm, length_ref),
            )
        )
    ]
    for copy in copies:
        copy.start()
    rows, width = residue_ref.shape
    blocks = rows // BLOCK
    inner = q.shape[1]
    copies[0].wait()
    copies[1].wait()
    gain = gain_ref[...]
    for b in range(blocks):
        span = slice(b * BLOCK, (b + 1) * BLOCK)
        normed[span, :] = rms_scaled(residue_ref[span, :].astype(F32), gain)
    for copy, weight, result in zip(copies[2:5], (wq, wk, wv), (q, k, v)):
        copy.wait()

        result[...] = dot(normed[...], weight[...]).astype(BF16)

    copies[6].wait()
    copies[7].wait()
    ids, live = block_facts(blocks, protein_ref, length_ref)
    lane = lax.broadcasted_iota(jnp.int32, (1, BLOCK), 1)
    mates, limits = [], []
    for b in range(blocks):
        mate, limit = jnp.int32(b), jnp.int32(0)
        for other in (b - 1, b + 1):
            if 0 <= other < blocks:
                same = ids[other] == ids[b]
                mate = jnp.where(same, other, mate)
                limit = jnp.where(same, live[other], limit)
        mates.append(mate)
        limits.append(limit)
    seen = [
        jnp.concatenate(
            [jnp.broadcast_to(lane < limit, (BLOCK, BLOCK)) for limit in (live[b], limits[b])], axis=1
        )
        for b in range(blocks)
    ]
    ones = jnp.ones((2 * BLOCK, HEAD_DIM), BF16)

    for h in range(inner // HEAD_DIM):
        cols = slice(h * HEAD_DIM, (h + 1) * HEAD_DIM)
        for b in range(blocks):
            span = slice(b * BLOCK, (b + 1) * BLOCK)
            mate = pl.ds(pl.multiple_of(mates[b] * BLOCK, BLOCK), BLOCK)
            window = jnp.concatenate([k[span, cols], k[mate, cols]], axis=0)
            scores = jnp.where(seen[b], dot_t(q[span, cols], window), MASKED_RAW)
            top = jnp.max(scores, axis=1, keepdims=True)
            weights = jnp.exp2((scores - top) * (SCALE * LOG2E)).astype(BF16)
            window = jnp.concatenate([v[span, cols], v[mate, cols]], axis=0)
            mixed = dot(weights, jnp.concatenate([window, ones], axis=1))
            context[span, cols] = (mixed[:, :HEAD_DIM] / mixed[:, HEAD_DIM:]).astype(BF16)

    copies[5].wait()
    half = width // 2
    stores = []
    for n in range(2):
        span = slice(n * half, (n + 1) * half)
        out_ref[span, :] = dot(context[...], wo[:, span]).astype(BF16).T
        stores.append(pltpu.make_async_copy(out_ref.at[span], out_hbm.at[span], sems.at[8 + n]))
        stores[n].start()
    for store in stores:
        store.wait()


def encoder(protein, length, residues, gain, wq, wk, wv, wo):
    rows, width = residues.shape
    inner = wq.shape[1]
    return pl.pallas_call(
        encoder_kernel,
        out_shape=jax.ShapeDtypeStruct((width, rows), BF16),
        in_specs=[ANY] * 8,
        out_specs=ANY,
        scratch_shapes=[
            pltpu.SMEM(protein.shape, jnp.int32),
            pltpu.SMEM(length.shape, jnp.int32),
            pltpu.VMEM((rows, width), BF16),
            pltpu.VMEM((1, width), F32),
            pltpu.VMEM((width, rows), BF16),
        ]
        + [pltpu.VMEM((width, inner), BF16)] * 3
        + [pltpu.VMEM((inner, width), BF16), pltpu.VMEM((rows, width), BF16)]
        + [pltpu.VMEM((rows, inner), BF16)] * 4
        + [pltpu.SemaphoreType.DMA((10,))],
        compiler_params=pltpu.CompilerParams(vmem_limit_bytes=VMEM_ALL),
        cost_estimate=pl.CostEstimate(
            flops=2 * rows * width * inner * 4, bytes_accessed=8 * width * inner, transcendentals=rows * rows * 8
        ),
        name="encoder",
    )(protein, length, residues, gain, wq, wk, wv, wo)


def as_column(row):
    size = row.shape[1]
    down = lax.broadcasted_iota(jnp.int32, (size, size), 0)
    along = lax.broadcasted_iota(jnp.int32, (size, size), 1)
    return jnp.sum(jnp.where(down == along, row, 0.0), axis=1, keepdims=True)


def query_kernel(
    protein_ref,
    length_ref,
    group_ref,
    where_ref,
    state_ref,
    dec_gain_ref,
    final_gain_ref,
    id_ref,
    wq_ref,
    wk_ref,
    wv_ref,
    residue_hbm,
    out_ref,
    back_ref,
    sorted_ref,
    gained_ref,
    own_ref,
    key_id_ref,
    table_ref,
    start_ref,
    key_weight,
    columns,
    turned,
    sem,
):
    rows, width = state_ref.shape
    features = own_ref.shape[0]
    here = where_ref[0]
    lanes = pl.ds(pl.multiple_of(here * features // BLOCK * BLOCK, BLOCK), BLOCK)
    copy = pltpu.make_async_copy(residue_hbm.at[:, lanes], columns, sem)
    copy.start()

    blocks = protein_ref.shape[0]
    slots = table_ref.shape[0]
    groups = key_id_ref.shape[0]
    each = slots // groups
    dest = [group_ref[protein_ref[b]] for b in range(blocks)]
    for s in range(slots):
        table_ref[s] = 0
    for b in range(blocks):
        rank = jnp.int32(0)
        for other in range(b):
            rank += jnp.where(dest[other] == dest[b], 1, 0)
        table_ref[dest[b] * each + rank] = b

    lane = lax.broadcasted_iota(jnp.int32, (1, BLOCK), 1)
    proteins = length_ref.shape[0] // groups
    for e in range(groups):
        taken = jnp.int32(0)
        names, limits = [jnp.int32(-1)] * each, [jnp.int32(0)] * each
        for p in range(e * proteins, (e + 1) * proteins):
            size = length_ref[p]
            count = lax.shift_right_logical(size + (BLOCK - 1), 7)
            wanted = group_ref[p] == where_ref[1]
            for s in range(each):
                offset = s - taken
                here_too = wanted & (offset >= 0) & (offset < count)
                names[s] = jnp.where(here_too, p, names[s])
                limits[s] = jnp.where(here_too, jnp.clip(size - offset * BLOCK, 0, BLOCK), limits[s])
            taken += jnp.where(wanted, count, 0)
        for s in range(each):
            key_id_ref[e, :, s * BLOCK : (s + 1) * BLOCK] = jnp.where(lane < limits[s], names[s], -1).astype(F32)

    id_row = id_ref[...].astype(F32)
    for e in range(start_ref.shape[0]):
        start_ref[e] = jnp.sum((id_row < 4.0 * e).astype(F32)).astype(jnp.int32)

    id_col = as_column(id_row)
    down = lax.broadcasted_iota(jnp.int32, (rows, rows), 0)
    along = lax.broadcasted_iota(jnp.int32, (rows, rows), 1)
    before = (id_col < id_row) | ((id_col == id_row) & (down < along))
    place_row = jnp.sum(before.astype(F32), axis=0, keepdims=True).astype(jnp.int32)
    before = (id_row < id_col) | ((id_row == id_col) & (along < down))
    place_col = jnp.sum(before.astype(F32), axis=1, keepdims=True).astype(jnp.int32)
    chosen = down == place_row
    back_ref[...] = (along == place_col).astype(F32).astype(BF16)
    sorted_ref[...] = jnp.sum(jnp.where(chosen, id_row, 0.0), axis=1, keepdims=True)
    normed = rms_scaled(state_ref[...].astype(F32), dec_gain_ref[...])
    normed = dot(chosen.astype(F32).astype(BF16), normed).astype(BF16)

    masks = origin_masks()
    part = features // CHAINS
    gain_parts = [
        as_column(final_gain_ref[:, c * BLOCK : (c + 1) * BLOCK]) for c in range(width // BLOCK)
    ]
    gain_ref = turned
    for c, gain in enumerate(gain_parts):
        gain_ref[c * BLOCK : (c + 1) * BLOCK, :] = gain
    for index in range(width // part):
        origin = here ^ int(masks[index])
        rows_from = pl.ds(
            pl.multiple_of(origin * features + index // (width // features) * part, part), part
        )
        half, chunk = divmod(index, width // features)
        far, chunk = divmod(chunk, width // features // 2)
        place = (far * CHAINS + half) * (width // features // 2) + chunk
        rows_to = slice(place * part, (place + 1) * part)
        gain = gain_ref[rows_from, :]
        key_weight[rows_to, :] = (wk_ref[rows_from, :].astype(F32) * gain).astype(BF16)
        gained_ref[rows_to, :] = (wv_ref[rows_from, :].astype(F32) * gain).astype(BF16)
    for pair in range(wq_ref.shape[1] // 256):
        queries = dot(normed, wq_ref[:, pair * 256 : (pair + 1) * 256]).astype(BF16)
        for side in range(2):
            h = pair * 2 + side
            head = queries[:, side * HEAD_DIM : (side + 1) * HEAD_DIM]
            out_ref[h] = dot_t(head, key_weight[:, h * HEAD_DIM : (h + 1) * HEAD_DIM]).astype(BF16)

    copy.wait()
    flipped = columns[...].astype(F32).T
    odd = here * features % BLOCK > 0
    own_ref[...] = jnp.where(odd, flipped[features:], flipped[:features])


def query_side(protein, length, group, where, states, dec_gain, final_gain, ids, wq, wk, wv, residues, groups):
    rows, width = states.shape
    inner = wq.shape[1]
    heads = inner // HEAD_DIM
    tokens = residues.shape[0]
    features = BLOCK // 2
    slots = groups * (tokens // BLOCK // 2)
    return pl.pallas_call(
        query_kernel,
        out_shape=(
            jax.ShapeDtypeStruct((heads, rows, width), BF16),
            jax.ShapeDtypeStruct((rows, rows), BF16),
            jax.ShapeDtypeStruct((rows, 1), F32),
            jax.ShapeDtypeStruct((width, inner), BF16),
            jax.ShapeDtypeStruct((features, tokens), F32),
            jax.ShapeDtypeStruct((groups, 1, slots // groups * BLOCK), F32),
            jax.ShapeDtypeStruct((slots,), jnp.int32),
            jax.ShapeDtypeStruct((groups + 1,), jnp.int32),
        ),
        in_specs=[SMEM] * 4 + [VMEM] * 7 + [ANY],
        out_specs=(VMEM,) * 6 + (SMEM,) * 2,
        scratch_shapes=[
            pltpu.VMEM((width, inner), BF16),
            pltpu.VMEM((tokens, BLOCK), BF16),
            pltpu.VMEM((width, 1), F32),
            pltpu.SemaphoreType.DMA,
        ],
        compiler_params=pltpu.CompilerParams(vmem_limit_bytes=VMEM_LIMIT),
        cost_estimate=pl.CostEstimate(
            flops=4 * rows * width * inner, bytes_accessed=6 * width * inner + 2 * heads * rows * width, transcendentals=0
        ),
        name="query_side",
    )(
        protein,
        length,
        group,
        where,
        states,
        dec_gain.reshape(1, width),
        final_gain.reshape(1, width),
        ids.reshape(1, rows),
        wq,
        wk,
        wv,
        residues,
    )


def placing_kernel(table_ref, arrived_ref, own_ref, encoded_ref, placed_ref):
    groups = placed_ref.shape[0]
    each = placed_ref.shape[2] // BLOCK
    sums = own_ref[...]
    for s in range(arrived_ref.shape[0]):
        sums = sums + arrived_ref[s].astype(F32)
    encoded_ref[...] = sums.astype(BF16)
    for d in range(groups):
        for s in range(each):
            start = pl.multiple_of(table_ref[d * each + s] * BLOCK, BLOCK)
            placed_ref[d, :, s * BLOCK : (s + 1) * BLOCK] = encoded_ref[:, pl.ds(start, BLOCK)]


def placing(table, arrived, own, groups):
    _, features, rows = arrived.shape
    each = table.shape[0] // groups
    return pl.pallas_call(
        placing_kernel,
        out_shape=(
            jax.ShapeDtypeStruct((features, rows), BF16),
            jax.ShapeDtypeStruct((groups, features, each * BLOCK), BF16),
        ),
        in_specs=[SMEM, VMEM, VMEM],
        out_specs=(VMEM, VMEM),
        compiler_params=pltpu.CompilerParams(vmem_limit_bytes=VMEM_PLACING),
        name="placing",
    )(table, arrived, own)


ROW_TILE = 32
TOGETHER = 4


def stacked(pieces, e):
    chunks, _, part, span = pieces[0].shape
    return jnp.concatenate([piece[:, e].reshape(chunks * part, span) for piece in pieces], axis=0)


def square_sums(pieces, e):
    chunks, _, part, span = pieces[0].shape
    squares = jnp.zeros((8, span), F32)
    for piece in pieces:
        for j in range(chunks):
            values = piece[j, e].astype(F32)
            squares = squares + jnp.sum((values * values).reshape(part // 8, 8, span), axis=0)
    return squares


def tile_spot(i):
    return pl.ds(pl.multiple_of(i * ROW_TILE, ROW_TILE), ROW_TILE)


def near_kernel(start_ref, query_ref, *refs):
    pieces, (score_ref, square_ref, work_ref) = refs[:CHAINS], refs[CHAINS:]
    heads, rows, _ = query_ref.shape
    groups = pieces[0].shape[1]
    near = CHAINS * pieces[0].shape[0] * pieces[0].shape[2]
    flat = heads * ROW_TILE
    room = (work_ref.shape[0] - 1) // 2

    def listed(e, count):
        first = start_ref[e] // ROW_TILE
        last = jnp.where(start_ref[e + 1] > start_ref[e], (start_ref[e + 1] + ROW_TILE - 1) // ROW_TILE, first)

        def note(i, at):
            work_ref[at] = e
            work_ref[room + at] = i
            return at + 1

        return lax.fori_loop(first, last, note, count)

    items = lax.fori_loop(0, groups, listed, jnp.int32(0))
    for extra in range(TOGETHER - 1):
        work_ref[items + extra] = work_ref[items - 1]
        work_ref[room + items + extra] = work_ref[room + items - 1]
    work_ref[2 * room] = (items + TOGETHER - 1) // TOGETHER

    @pl.loop(0, groups)
    def _(e):
        square_ref[e] = square_sums(pieces, e)

    @pl.loop(0, work_ref[2 * room])
    def _(n):
        for a in range(TOGETHER):
            e, i = work_ref[n * TOGETHER + a], work_ref[room + n * TOGETHER + a]
            query = query_ref[:, tile_spot(i), 0:near].reshape(flat, near)
            score_ref[n * TOGETHER + a] = dot(query, stacked(pieces, e))


def work_room(rows, groups):
    return rows // ROW_TILE + groups + TOGETHER


def near_scores(starts, queries, pieces):
    heads, rows, width = queries.shape
    groups, span = pieces[0].shape[1], pieces[0].shape[3]
    flat = heads * ROW_TILE
    most = rows // ROW_TILE + groups - 1
    most = -(-most // TOGETHER) * TOGETHER
    return pl.pallas_call(
        near_kernel,
        out_shape=(
            jax.ShapeDtypeStruct((most, flat, span), F32),
            jax.ShapeDtypeStruct((groups, 8, span), F32),
            jax.ShapeDtypeStruct((2 * work_room(rows, groups) + 1,), jnp.int32),
        ),
        in_specs=[SMEM] + [VMEM] * (1 + CHAINS),
        out_specs=(VMEM, VMEM, SMEM),
        compiler_params=pltpu.CompilerParams(vmem_limit_bytes=VMEM_NEAR),
        cost_estimate=pl.CostEstimate(
            flops=most * flat * span * width, bytes_accessed=4 * most * flat * span, transcendentals=0
        ),
        name="near_scores",
    )(starts, queries, *pieces)


def cross_kernel(
    work_hbm,
    query_ref,
    score_ref,
    square_ref,
    id_ref,
    key_id_ref,
    back_ref,
    wv_ref,
    wo_ref,
    *refs,
):
    pieces, rest = refs[: 2 * CHAINS], refs[2 * CHAINS :]
    out_hbm, out_ref, work_ref, key_scale, mixed, context, sems = rest
    work_copy = pltpu.make_async_copy(work_hbm, work_ref, sems.at[0])
    work_copy.start()
    heads, rows, width = query_ref.shape
    chunks, groups, part, span = pieces[0].shape
    near = CHAINS * chunks * part
    room = (work_ref.shape[0] - 1) // 2

    @pl.loop(0, groups)
    def _(e):
        squares = square_ref[e] + square_sums(pieces[CHAINS:], e)
        total = jnp.sum(squares, axis=0, keepdims=True)
        key_scale[e] = lax.rsqrt(total / width + EPSILON)

    work_copy.wait()
    flat = heads * ROW_TILE

    @pl.loop(0, work_ref[2 * room])
    def _(n):
        numbers = [n * TOGETHER + a for a in range(TOGETHER)]
        todo = [(work_ref[at], work_ref[room + at]) for at in numbers]
        spots = [tile_spot(i) for _, i in todo]
        scores = [
            dot(query_ref[:, at, near:].reshape(flat, width - near), stacked(pieces[CHAINS:], e)) + score_ref[number]
            for (e, _), at, number in zip(todo, spots, numbers)
        ]
        weights = []
        for (e, _), at, raw in zip(todo, spots, scores):
            scale = key_scale[e]
            seen = id_ref[at, :] == key_id_ref[e]
            raw = (raw * (scale * (SCALE * LOG2E))).reshape(heads, ROW_TILE, span)
            raw = jnp.where(seen[None], raw, MASKED_LOG2)
            expo = jnp.exp2(raw - jnp.max(raw, axis=2, keepdims=True))
            share = 1.0 / jnp.sum(expo, axis=2, keepdims=True)
            weights.append((expo * scale[None] * share).astype(BF16).reshape(flat, span))
        spreads = [dot_t(w, stacked(pieces, e)) for w, (e, _) in zip(weights, todo)]
        for (e, _), at, spread in zip(todo, spots, spreads):
            ids = id_ref[at, :]
            mine = (ids >= (e * 4).astype(F32)) & (ids < (e * 4 + 4).astype(F32))
            spread = spread.astype(BF16).reshape(heads, ROW_TILE, width)
            mixed[:, at, :] = jnp.where(mine[None], spread, mixed[:, at, :])

    for h in range(heads):
        cols = slice(h * HEAD_DIM, (h + 1) * HEAD_DIM)
        context[:, cols] = dot(mixed[h], wv_ref[:, cols]).astype(BF16)

    context[...] = dot(back_ref[...], context[...]).astype(BF16)

    half = rows // 2
    stores = []
    for n in range(2):
        span = slice(n * half, (n + 1) * half)
        out_ref[span, :] = dot(context[span, :], wo_ref[...]).astype(BF16)
        stores.append(pltpu.make_async_copy(out_ref.at[span], out_hbm.at[span], sems.at[1 + n]))
        stores[n].start()
    for store in stores:
        store.wait()


def cross(work, queries, scores, squares, ids, key_ids, back, pieces, wv, wo):
    heads, rows, width = queries.shape
    groups, span = key_ids.shape[0], key_ids.shape[2]
    inner = wv.shape[1]
    return pl.pallas_call(
        cross_kernel,
        out_shape=jax.ShapeDtypeStruct((rows, width), BF16),
        in_specs=[ANY] + [VMEM] * (8 + 2 * CHAINS),
        out_specs=ANY,
        scratch_shapes=[
            pltpu.VMEM((rows, width), BF16),
            pltpu.SMEM(work.shape, jnp.int32),
            pltpu.VMEM((groups, 1, span), F32),
            pltpu.VMEM((heads, rows, width), BF16),
            pltpu.VMEM((rows, inner), BF16),
            pltpu.SemaphoreType.DMA((3,)),
        ],
        compiler_params=pltpu.CompilerParams(vmem_limit_bytes=VMEM_LIMIT),
        cost_estimate=pl.CostEstimate(
            flops=8 * rows * width * inner, bytes_accessed=2 * groups * width * span, transcendentals=rows * span * heads
        ),
        name="cross",
    )(work, queries, scores, squares, ids, key_ids, back, wv, wo, *pieces)


def exchange(x, groups, tensor, chain, step):
    pairs = [(d * tensor + t, d * tensor + (t ^ ORDERS[chain][step])) for d in range(groups) for t in range(tensor)]
    return lax.ppermute(x, ("dp", "tensor"), pairs)


def gathered(x, groups, tensor):
    part = x.shape[1] // CHAINS
    held = [x[None, :, c * part : (c + 1) * part] for c in range(CHAINS)]
    for step in range(3):
        got = [exchange(held[c], groups, tensor, c, step) for c in range(CHAINS)]
        held = [jnp.concatenate([held[c], got[c]], axis=0) for c in range(CHAINS)]
    got = [exchange(held[c], groups, tensor, c, 3) for c in range(CHAINS)]
    return held, got


def origin_masks():
    table = np.zeros((CHAINS, 16), np.int32)
    for chain in range(CHAINS):
        for j in range(16):
            for step in range(4):
                if j >> step & 1:
                    table[chain, j] ^= ORDERS[chain][step]
    return table.reshape(-1)


def body(
    residues,
    block_protein,
    protein_length,
    decoder_group,
    enc_gain,
    enc_query,
    enc_key,
    enc_value,
    enc_out,
    decoder_states,
    query_protein,
    dec_gain,
    final_gain,
    cross_query,
    cross_key,
    cross_value,
    cross_out,
):
    groups = lax.axis_size("dp")
    tensor = lax.axis_size("tensor")
    dp_index = lax.axis_index("dp")
    tensor_index = lax.axis_index("tensor")
    rows, width = residues.shape
    query_rows = decoder_states.shape[0]
    slice_width = width // tensor

    partial_sums = encoder(
        block_protein, protein_length, residues, enc_gain.reshape(1, width), enc_query, enc_key, enc_value, enc_out
    )
    arrived = lax.all_to_all(
        partial_sums.reshape(tensor, slice_width, rows), "tensor", split_axis=0, concat_axis=0, tiled=True
    )
    where = jnp.stack([tensor_index, dp_index]).astype(jnp.int32)
    queries, back, sorted_ids, gained_value, own, key_ids, table, starts = query_side(
        block_protein,
        protein_length,
        decoder_group,
        where,
        decoder_states,
        dec_gain,
        final_gain,
        query_protein,
        cross_query,
        cross_key,
        cross_value,
        residues,
        groups,
    )
    share = query_rows // tensor
    own_rows = lax.dynamic_slice_in_dim(decoder_states, tensor_index * share, share, 0).astype(F32)
    arrived, own, queries = lax.optimization_barrier((arrived, own, queries))
    encoded, placed = placing(table, arrived, own, groups)
    received = lax.all_to_all(placed, "dp", split_axis=0, concat_axis=0, tiled=True)
    near, far = gathered(received, groups, tensor)
    scores, squares, work = near_scores(starts, queries, near)
    outcome = cross(
        work, queries, scores, squares, sorted_ids, key_ids, back, (*near, *far), gained_value, cross_out
    )
    mixed = lax.all_to_all(
        outcome.reshape(tensor, share, width), "tensor", split_axis=0, concat_axis=0, tiled=True
    )
    mixed, own_rows = lax.optimization_barrier((mixed, own_rows))
    mixed = mixed.astype(F32).sum(axis=0)
    decoded = (own_rows + mixed).astype(BF16)
    return (encoded.T, decoded)


def solution(mesh):
    in_specs = (
        P("dp", None),
        P("dp"),
        P(),
        P(),
        P(),
        P(None, "tensor"),
        P(None, "tensor"),
        P(None, "tensor"),
        P("tensor", None),
        P("dp", None),
        P("dp"),
        P(),
        P(),
        P(None, "tensor"),
        P(None, "tensor"),
        P(None, "tensor"),
        P("tensor", None),
    )
    out_specs = (P("dp", "tensor"), P(("dp", "tensor"), None))
    return jax.shard_map(body, mesh=mesh, in_specs=in_specs, out_specs=out_specs, check_vma=False)
```

```python
import jax
import jax.numpy as jnp
import numpy as np
from jax import lax
from jax.experimental import pallas as pl
from jax.experimental.pallas import tpu as pltpu
from jax.sharding import PartitionSpec as P

HEAD_DIM = 128
BLOCK = 128
EPSILON = 1e-06
MASKED = -1000000000.0
SCALE = HEAD_DIM ** (-0.5)
LOG2E = 1.4426950408889634
BF16 = jnp.bfloat16
F32 = jnp.float32
MASKED_RAW = MASKED / SCALE
MASKED_LOG2 = MASKED * LOG2E
VMEM_LIMIT = 32 * 1024 * 1024
VMEM_ALL = 60 * 1024 * 1024
VMEM_NEAR = 24 * 1024 * 1024
VMEM_PLACING = 8 * 1024 * 1024

VMEM = pl.BlockSpec(memory_space=pltpu.VMEM)
SMEM = pl.BlockSpec(memory_space=pltpu.SMEM)
ANY = pl.BlockSpec(memory_space=pl.ANY)

XA, XB, YA, YB = 1, 3, 4, 12
ORDERS = ((XA, YA, XB, YB), (YA, XA, YB, XB), (XB, YB, XA, YA), (YB, XB, YA, XA))
CHAINS = len(ORDERS)


def rms_scaled(x, gain):
    scale = lax.rsqrt(jnp.mean(x * x, axis=1, keepdims=True) + EPSILON)
    return (x * scale * gain).astype(BF16)


def dot(a, b):
    return jnp.dot(a, b, preferred_element_type=F32)


def dot_t(a, b):
    return lax.dot_general(a, b, (((1,), (1,)), ((), ())), preferred_element_type=F32)


def block_facts(blocks, protein_ref, length_ref):
    ids = [protein_ref[b] for b in range(blocks)]
    live = []
    for b in range(blocks):
        offset = jnp.int32(0)
        for other in range(b):
            offset += jnp.where(ids[other] == ids[b], BLOCK, 0)
        live.append(jnp.clip(length_ref[ids[b]] - offset, 0, BLOCK))
    return ids, live


def encoder_kernel(
    protein_hbm,
    length_hbm,
    residue_hbm,
    gain_hbm,
    wq_hbm,
    wk_hbm,
    wv_hbm,
    wo_hbm,
    out_hbm,
    protein_ref,
    length_ref,
    residue_ref,
    gain_ref,
    out_ref,
    wq,
    wk,
    wv,
    wo,
    normed,
    q,
    k,
    v,
    context,
    sems,
):
    copies = [
        pltpu.make_async_copy(src, dst, sems.at[i])
        for i, (src, dst) in enumerate(
            (
                (gain_hbm, gain_ref),
                (residue_hbm, residue_ref),
                (wq_hbm, wq),
                (wk_hbm, wk),
                (wv_hbm, wv),
                (wo_hbm, wo),
                (protein_hbm, protein_ref),
                (length_hbm, length_ref),
            )
        )
    ]
    for copy in copies:
        copy.start()
    rows, width = residue_ref.shape
    blocks = rows // BLOCK
    inner = q.shape[1]
    copies[0].wait()
    copies[1].wait()
    gain = gain_ref[...]
    for b in range(blocks):
        span = slice(b * BLOCK, (b + 1) * BLOCK)
        normed[span, :] = rms_scaled(residue_ref[span, :].astype(F32), gain)
    for copy, weight, result in zip(copies[2:5], (wq, wk, wv), (q, k, v)):
        copy.wait()

        result[...] = dot(normed[...], weight[...]).astype(BF16)

    copies[6].wait()
    copies[7].wait()
    ids, live = block_facts(blocks, protein_ref, length_ref)
    lane = lax.broadcasted_iota(jnp.int32, (1, BLOCK), 1)
    mates, limits = [], []
    for b in range(blocks):
        mate, limit = jnp.int32(b), jnp.int32(0)
        for other in (b - 1, b + 1):
            if 0 <= other < blocks:
                same = ids[other] == ids[b]
                mate = jnp.where(same, other, mate)
                limit = jnp.where(same, live[other], limit)
        mates.append(mate)
        limits.append(limit)
    seen = [
        jnp.concatenate(
            [jnp.broadcast_to(lane < limit, (BLOCK, BLOCK)) for limit in (live[b], limits[b])], axis=1
        )
        for b in range(blocks)
    ]
    ones = jnp.ones((2 * BLOCK, HEAD_DIM), BF16)

    for h in range(inner // HEAD_DIM):
        cols = slice(h * HEAD_DIM, (h + 1) * HEAD_DIM)
        for b in range(blocks):
            span = slice(b * BLOCK, (b + 1) * BLOCK)
            mate = pl.ds(pl.multiple_of(mates[b] * BLOCK, BLOCK), BLOCK)
            window = jnp.concatenate([k[span, cols], k[mate, cols]], axis=0)
            scores = jnp.where(seen[b], dot_t(q[span, cols], window), MASKED_RAW)
            top = jnp.max(scores, axis=1, keepdims=True)
            weights = jnp.exp2((scores - top) * (SCALE * LOG2E)).astype(BF16)
            window = jnp.concatenate([v[span, cols], v[mate, cols]], axis=0)
            mixed = dot(weights, jnp.concatenate([window, ones], axis=1))
            context[span, cols] = (mixed[:, :HEAD_DIM] / mixed[:, HEAD_DIM:]).astype(BF16)

    copies[5].wait()
    half = width // 2
    stores = []
    for n in range(2):
        span = slice(n * half, (n + 1) * half)
        out_ref[span, :] = dot(context[...], wo[:, span]).astype(BF16).T
        stores.append(pltpu.make_async_copy(out_ref.at[span], out_hbm.at[span], sems.at[8 + n]))
        stores[n].start()
    for store in stores:
        store.wait()


def encoder(protein, length, residues, gain, wq, wk, wv, wo):
    rows, width = residues.shape
    inner = wq.shape[1]
    return pl.pallas_call(
        encoder_kernel,
        out_shape=jax.ShapeDtypeStruct((width, rows), BF16),
        in_specs=[ANY] * 8,
        out_specs=ANY,
        scratch_shapes=[
            pltpu.SMEM(protein.shape, jnp.int32),
            pltpu.SMEM(length.shape, jnp.int32),
            pltpu.VMEM((rows, width), BF16),
            pltpu.VMEM((1, width), F32),
            pltpu.VMEM((width, rows), BF16),
        ]
        + [pltpu.VMEM((width, inner), BF16)] * 3
        + [pltpu.VMEM((inner, width), BF16), pltpu.VMEM((rows, width), BF16)]
        + [pltpu.VMEM((rows, inner), BF16)] * 4
        + [pltpu.SemaphoreType.DMA((10,))],
        compiler_params=pltpu.CompilerParams(vmem_limit_bytes=VMEM_ALL),
        cost_estimate=pl.CostEstimate(
            flops=2 * rows * width * inner * 4, bytes_accessed=8 * width * inner, transcendentals=rows * rows * 8
        ),
        name="encoder",
    )(protein, length, residues, gain, wq, wk, wv, wo)


def as_column(row):
    size = row.shape[1]
    down = lax.broadcasted_iota(jnp.int32, (size, size), 0)
    along = lax.broadcasted_iota(jnp.int32, (size, size), 1)
    return jnp.sum(jnp.where(down == along, row, 0.0), axis=1, keepdims=True)


def query_kernel(
    protein_ref,
    length_ref,
    group_ref,
    where_ref,
    state_ref,
    dec_gain_ref,
    final_gain_ref,
    id_ref,
    wq_ref,
    wk_ref,
    wv_ref,
    residue_hbm,
    out_ref,
    back_ref,
    sorted_ref,
    gained_ref,
    own_ref,
    key_id_ref,
    table_ref,
    start_ref,
    key_weight,
    columns,
    turned,
    sem,
):
    rows, width = state_ref.shape
    features = own_ref.shape[0]
    here = where_ref[0]
    lanes = pl.ds(pl.multiple_of(here * features // BLOCK * BLOCK, BLOCK), BLOCK)
    copy = pltpu.make_async_copy(residue_hbm.at[:, lanes], columns, sem)
    copy.start()

    blocks = protein_ref.shape[0]
    slots = table_ref.shape[0]
    groups = key_id_ref.shape[0]
    each = slots // groups
    dest = [group_ref[protein_ref[b]] for b in range(blocks)]
    for s in range(slots):
        table_ref[s] = 0
    for b in range(blocks):
        rank = jnp.int32(0)
        for other in range(b):
            rank += jnp.where(dest[other] == dest[b], 1, 0)
        table_ref[dest[b] * each + rank] = b

    lane = lax.broadcasted_iota(jnp.int32, (1, BLOCK), 1)
    proteins = length_ref.shape[0] // groups
    for e in range(groups):
        taken = jnp.int32(0)
        names, limits = [jnp.int32(-1)] * each, [jnp.int32(0)] * each
        for p in range(e * proteins, (e + 1) * proteins):
            size = length_ref[p]
            count = lax.shift_right_logical(size + (BLOCK - 1), 7)
            wanted = group_ref[p] == where_ref[1]
            for s in range(each):
                offset = s - taken
                here_too = wanted & (offset >= 0) & (offset < count)
                names[s] = jnp.where(here_too, p, names[s])
                limits[s] = jnp.where(here_too, jnp.clip(size - offset * BLOCK, 0, BLOCK), limits[s])
            taken += jnp.where(wanted, count, 0)
        for s in range(each):
            key_id_ref[e, :, s * BLOCK : (s + 1) * BLOCK] = jnp.where(lane < limits[s], names[s], -1).astype(F32)

    id_row = id_ref[...].astype(F32)
    for e in range(start_ref.shape[0]):
        start_ref[e] = jnp.sum((id_row < 4.0 * e).astype(F32)).astype(jnp.int32)

    id_col = as_column(id_row)
    down = lax.broadcasted_iota(jnp.int32, (rows, rows), 0)
    along = lax.broadcasted_iota(jnp.int32, (rows, rows), 1)
    before = (id_col < id_row) | ((id_col == id_row) & (down < along))
    place_row = jnp.sum(before.astype(F32), axis=0, keepdims=True).astype(jnp.int32)
    before = (id_row < id_col) | ((id_row == id_col) & (along < down))
    place_col = jnp.sum(before.astype(F32), axis=1, keepdims=True).astype(jnp.int32)
    chosen = down == place_row
    back_ref[...] = (along == place_col).astype(F32).astype(BF16)
    sorted_ref[...] = jnp.sum(jnp.where(chosen, id_row, 0.0), axis=1, keepdims=True)
    normed = rms_scaled(state_ref[...].astype(F32), dec_gain_ref[...])
    normed = dot(chosen.astype(F32).astype(BF16), normed).astype(BF16)

    masks = origin_masks()
    part = features // CHAINS
    gain_parts = [
        as_column(final_gain_ref[:, c * BLOCK : (c + 1) * BLOCK]) for c in range(width // BLOCK)
    ]
    gain_ref = turned
    for c, gain in enumerate(gain_parts):
        gain_ref[c * BLOCK : (c + 1) * BLOCK, :] = gain
    for index in range(width // part):
        origin = here ^ int(masks[index])
        rows_from = pl.ds(
            pl.multiple_of(origin * features + index // (width // features) * part, part), part
        )
        half, chunk = divmod(index, width // features)
        far, chunk = divmod(chunk, width // features // 2)
        place = (far * CHAINS + half) * (width // features // 2) + chunk
        rows_to = slice(place * part, (place + 1) * part)
        gain = gain_ref[rows_from, :]
        key_weight[rows_to, :] = (wk_ref[rows_from, :].astype(F32) * gain).astype(BF16)
        gained_ref[rows_to, :] = (wv_ref[rows_from, :].astype(F32) * gain).astype(BF16)
    for pair in range(wq_ref.shape[1] // 256):
        queries = dot(normed, wq_ref[:, pair * 256 : (pair + 1) * 256]).astype(BF16)
        for side in range(2):
            h = pair * 2 + side
            head = queries[:, side * HEAD_DIM : (side + 1) * HEAD_DIM]
            out_ref[h] = dot_t(head, key_weight[:, h * HEAD_DIM : (h + 1) * HEAD_DIM]).astype(BF16)

    copy.wait()
    flipped = columns[...].astype(F32).T
    odd = here * features % BLOCK > 0
    own_ref[...] = jnp.where(odd, flipped[features:], flipped[:features])


def query_side(protein, length, group, where, states, dec_gain, final_gain, ids, wq, wk, wv, residues, groups):
    rows, width = states.shape
    inner = wq.shape[1]
    heads = inner // HEAD_DIM
    tokens = residues.shape[0]
    features = BLOCK // 2
    slots = groups * (tokens // BLOCK // 2)
    return pl.pallas_call(
        query_kernel,
        out_shape=(
            jax.ShapeDtypeStruct((heads, rows, width), BF16),
            jax.ShapeDtypeStruct((rows, rows), BF16),
            jax.ShapeDtypeStruct((rows, 1), F32),
            jax.ShapeDtypeStruct((width, inner), BF16),
            jax.ShapeDtypeStruct((features, tokens), F32),
            jax.ShapeDtypeStruct((groups, 1, slots // groups * BLOCK), F32),
            jax.ShapeDtypeStruct((slots,), jnp.int32),
            jax.ShapeDtypeStruct((groups + 1,), jnp.int32),
        ),
        in_specs=[SMEM] * 4 + [VMEM] * 7 + [ANY],
        out_specs=(VMEM,) * 6 + (SMEM,) * 2,
        scratch_shapes=[
            pltpu.VMEM((width, inner), BF16),
            pltpu.VMEM((tokens, BLOCK), BF16),
            pltpu.VMEM((width, 1), F32),
            pltpu.SemaphoreType.DMA,
        ],
        compiler_params=pltpu.CompilerParams(vmem_limit_bytes=VMEM_LIMIT),
        cost_estimate=pl.CostEstimate(
            flops=4 * rows * width * inner, bytes_accessed=6 * width * inner + 2 * heads * rows * width, transcendentals=0
        ),
        name="query_side",
    )(
        protein,
        length,
        group,
        where,
        states,
        dec_gain.reshape(1, width),
        final_gain.reshape(1, width),
        ids.reshape(1, rows),
        wq,
        wk,
        wv,
        residues,
    )


def placing_kernel(table_ref, arrived_ref, own_ref, encoded_ref, placed_ref):
    groups = placed_ref.shape[0]
    each = placed_ref.shape[2] // BLOCK
    sums = own_ref[...]
    for s in range(arrived_ref.shape[0]):
        sums = sums + arrived_ref[s].astype(F32)
    encoded_ref[...] = sums.astype(BF16)
    for d in range(groups):
        for s in range(each):
            start = pl.multiple_of(table_ref[d * each + s] * BLOCK, BLOCK)
            placed_ref[d, :, s * BLOCK : (s + 1) * BLOCK] = encoded_ref[:, pl.ds(start, BLOCK)]


def placing(table, arrived, own, groups):
    _, features, rows = arrived.shape
    each = table.shape[0] // groups
    return pl.pallas_call(
        placing_kernel,
        out_shape=(
            jax.ShapeDtypeStruct((features, rows), BF16),
            jax.ShapeDtypeStruct((groups, features, each * BLOCK), BF16),
        ),
        in_specs=[SMEM, VMEM, VMEM],
        out_specs=(VMEM, VMEM),
        compiler_params=pltpu.CompilerParams(vmem_limit_bytes=VMEM_PLACING),
        name="placing",
    )(table, arrived, own)


ROW_TILE = 32
TOGETHER = 4


def stacked(pieces, e):
    chunks, _, part, span = pieces[0].shape
    return jnp.concatenate([piece[:, e].reshape(chunks * part, span) for piece in pieces], axis=0)


def square_sums(pieces, e):
    chunks, _, part, span = pieces[0].shape
    squares = jnp.zeros((8, span), F32)
    for piece in pieces:
        for j in range(chunks):
            values = piece[j, e].astype(F32)
            squares = squares + jnp.sum((values * values).reshape(part // 8, 8, span), axis=0)
    return squares


def tile_spot(i):
    return pl.ds(pl.multiple_of(i * ROW_TILE, ROW_TILE), ROW_TILE)


def near_kernel(start_ref, query_ref, *refs):
    pieces, (score_ref, square_ref, work_ref) = refs[:CHAINS], refs[CHAINS:]
    heads, rows, _ = query_ref.shape
    groups = pieces[0].shape[1]
    near = CHAINS * pieces[0].shape[0] * pieces[0].shape[2]
    flat = heads * ROW_TILE
    room = (work_ref.shape[0] - 1) // 2

    def listed(e, count):
        first = start_ref[e] // ROW_TILE
        last = jnp.where(start_ref[e + 1] > start_ref[e], (start_ref[e + 1] + ROW_TILE - 1) // ROW_TILE, first)

        def note(i, at):
            work_ref[at] = e
            work_ref[room + at] = i
            return at + 1

        return lax.fori_loop(first, last, note, count)

    items = lax.fori_loop(0, groups, listed, jnp.int32(0))
    for extra in range(TOGETHER - 1):
        work_ref[items + extra] = work_ref[items - 1]
        work_ref[room + items + extra] = work_ref[room + items - 1]
    work_ref[2 * room] = (items + TOGETHER - 1) // TOGETHER

    @pl.loop(0, groups)
    def _(e):
        square_ref[e] = square_sums(pieces, e)

    @pl.loop(0, work_ref[2 * room])
    def _(n):
        for a in range(TOGETHER):
            e, i = work_ref[n * TOGETHER + a], work_ref[room + n * TOGETHER + a]
            query = query_ref[:, tile_spot(i), 0:near].reshape(flat, near)
            score_ref[n * TOGETHER + a] = dot(query, stacked(pieces, e))


def work_room(rows, groups):
    return rows // ROW_TILE + groups + TOGETHER


def near_scores(starts, queries, pieces):
    heads, rows, width = queries.shape
    groups, span = pieces[0].shape[1], pieces[0].shape[3]
    flat = heads * ROW_TILE
    most = rows // ROW_TILE + groups - 1
    most = -(-most // TOGETHER) * TOGETHER
    return pl.pallas_call(
        near_kernel,
        out_shape=(
            jax.ShapeDtypeStruct((most, flat, span), F32),
            jax.ShapeDtypeStruct((groups, 8, span), F32),
            jax.ShapeDtypeStruct((2 * work_room(rows, groups) + 1,), jnp.int32),
        ),
        in_specs=[SMEM] + [VMEM] * (1 + CHAINS),
        out_specs=(VMEM, VMEM, SMEM),
        compiler_params=pltpu.CompilerParams(vmem_limit_bytes=VMEM_NEAR),
        cost_estimate=pl.CostEstimate(
            flops=most * flat * span * width, bytes_accessed=4 * most * flat * span, transcendentals=0
        ),
        name="near_scores",
    )(starts, queries, *pieces)


def cross_kernel(
    work_hbm,
    query_ref,
    score_ref,
    square_ref,
    id_ref,
    key_id_ref,
    back_ref,
    wv_ref,
    wo_ref,
    *refs,
):
    pieces, rest = refs[: 2 * CHAINS], refs[2 * CHAINS :]
    out_hbm, out_ref, work_ref, key_scale, mixed, context, sems = rest
    work_copy = pltpu.make_async_copy(work_hbm, work_ref, sems.at[0])
    work_copy.start()
    heads, rows, width = query_ref.shape
    chunks, groups, part, span = pieces[0].shape
    near = CHAINS * chunks * part
    room = (work_ref.shape[0] - 1) // 2

    @pl.loop(0, groups)
    def _(e):
        squares = square_ref[e] + square_sums(pieces[CHAINS:], e)
        total = jnp.sum(squares, axis=0, keepdims=True)
        key_scale[e] = lax.rsqrt(total / width + EPSILON)

    work_copy.wait()
    flat = heads * ROW_TILE

    @pl.loop(0, work_ref[2 * room])
    def _(n):
        numbers = [n * TOGETHER + a for a in range(TOGETHER)]
        todo = [(work_ref[at], work_ref[room + at]) for at in numbers]
        spots = [tile_spot(i) for _, i in todo]
        scores = [
            dot(query_ref[:, at, near:].reshape(flat, width - near), stacked(pieces[CHAINS:], e)) + score_ref[number]
            for (e, _), at, number in zip(todo, spots, numbers)
        ]
        weights = []
        for (e, _), at, raw in zip(todo, spots, scores):
            scale = key_scale[e]
            seen = id_ref[at, :] == key_id_ref[e]
            raw = (raw * (scale * (SCALE * LOG2E))).reshape(heads, ROW_TILE, span)
            raw = jnp.where(seen[None], raw, MASKED_LOG2)
            expo = jnp.exp2(raw - jnp.max(raw, axis=2, keepdims=True))
            share = 1.0 / jnp.sum(expo, axis=2, keepdims=True)
            weights.append((expo * scale[None] * share).astype(BF16).reshape(flat, span))
        spreads = [dot_t(w, stacked(pieces, e)) for w, (e, _) in zip(weights, todo)]
        for (e, _), at, spread in zip(todo, spots, spreads):
            ids = id_ref[at, :]
            mine = (ids >= (e * 4).astype(F32)) & (ids < (e * 4 + 4).astype(F32))
            spread = spread.astype(BF16).reshape(heads, ROW_TILE, width)
            mixed[:, at, :] = jnp.where(mine[None], spread, mixed[:, at, :])

    for h in range(heads):
        cols = slice(h * HEAD_DIM, (h + 1) * HEAD_DIM)
        context[:, cols] = dot(mixed[h], wv_ref[:, cols]).astype(BF16)

    context[...] = dot(back_ref[...], context[...]).astype(BF16)

    half = rows // 2
    stores = []
    for n in range(2):
        span = slice(n * half, (n + 1) * half)
        out_ref[span, :] = dot(context[span, :], wo_ref[...]).astype(BF16)
        stores.append(pltpu.make_async_copy(out_ref.at[span], out_hbm.at[span], sems.at[1 + n]))
        stores[n].start()
    for store in stores:
        store.wait()


def cross(work, queries, scores, squares, ids, key_ids, back, pieces, wv, wo):
    heads, rows, width = queries.shape
    groups, span = key_ids.shape[0], key_ids.shape[2]
    inner = wv.shape[1]
    return pl.pallas_call(
        cross_kernel,
        out_shape=jax.ShapeDtypeStruct((rows, width), BF16),
        in_specs=[ANY] + [VMEM] * (8 + 2 * CHAINS),
        out_specs=ANY,
        scratch_shapes=[
            pltpu.VMEM((rows, width), BF16),
            pltpu.SMEM(work.shape, jnp.int32),
            pltpu.VMEM((groups, 1, span), F32),
            pltpu.VMEM((heads, rows, width), BF16),
            pltpu.VMEM((rows, inner), BF16),
            pltpu.SemaphoreType.DMA((3,)),
        ],
        compiler_params=pltpu.CompilerParams(vmem_limit_bytes=VMEM_LIMIT),
        cost_estimate=pl.CostEstimate(
            flops=8 * rows * width * inner, bytes_accessed=2 * groups * width * span, transcendentals=rows * span * heads
        ),
        name="cross",
    )(work, queries, scores, squares, ids, key_ids, back, wv, wo, *pieces)


def exchange(x, groups, tensor, chain, step):
    pairs = [(d * tensor + t, d * tensor + (t ^ ORDERS[chain][step])) for d in range(groups) for t in range(tensor)]
    return lax.ppermute(x, ("dp", "tensor"), pairs)


def gathered(x, groups, tensor):
    part = x.shape[1] // CHAINS
    held = [x[None, :, c * part : (c + 1) * part] for c in range(CHAINS)]
    for step in range(3):
        got = [exchange(held[c], groups, tensor, c, step) for c in range(CHAINS)]
        held = [jnp.concatenate([held[c], got[c]], axis=0) for c in range(CHAINS)]
    got = [exchange(held[c], groups, tensor, c, 3) for c in range(CHAINS)]
    return held, got


def origin_masks():
    table = np.zeros((CHAINS, 16), np.int32)
    for chain in range(CHAINS):
        for j in range(16):
            for step in range(4):
                if j >> step & 1:
                    table[chain, j] ^= ORDERS[chain][step]
    return table.reshape(-1)


def body(
    residues,
    block_protein,
    protein_length,
    decoder_group,
    enc_gain,
    enc_query,
    enc_key,
    enc_value,
    enc_out,
    decoder_states,
    query_protein,
    dec_gain,
    final_gain,
    cross_query,
    cross_key,
    cross_value,
    cross_out,
):
    groups = lax.axis_size("dp")
    tensor = lax.axis_size("tensor")
    dp_index = lax.axis_index("dp")
    tensor_index = lax.axis_index("tensor")
    rows, width = residues.shape
    query_rows = decoder_states.shape[0]
    slice_width = width // tensor

    partial_sums = encoder(
        block_protein, protein_length, residues, enc_gain.reshape(1, width), enc_query, enc_key, enc_value, enc_out
    )
    arrived = lax.all_to_all(
        partial_sums.reshape(tensor, slice_width, rows), "tensor", split_axis=0, concat_axis=0, tiled=True
    )
    where = jnp.stack([tensor_index, dp_index]).astype(jnp.int32)
    queries, back, sorted_ids, gained_value, own, key_ids, table, starts = query_side(
        block_protein,
        protein_length,
        decoder_group,
        where,
        decoder_states,
        dec_gain,
        final_gain,
        query_protein,
        cross_query,
        cross_key,
        cross_value,
        residues,
        groups,
    )
    share = query_rows // tensor
    own_rows = lax.dynamic_slice_in_dim(decoder_states, tensor_index * share, share, 0).astype(F32)
    arrived, own, queries = lax.optimization_barrier((arrived, own, queries))
    encoded, placed = placing(table, arrived, own, groups)
    received = lax.all_to_all(placed, "dp", split_axis=0, concat_axis=0, tiled=True)
    near, far = gathered(received, groups, tensor)
    scores, squares, work = near_scores(starts, queries, near)
    outcome = cross(
        work, queries, scores, squares, sorted_ids, key_ids, back, (*near, *far), gained_value, cross_out
    )
    mixed = lax.all_to_all(
        outcome.reshape(tensor, share, width), "tensor", split_axis=0, concat_axis=0, tiled=True
    )
    mixed, own_rows = lax.optimization_barrier((mixed, own_rows))
    mixed = mixed.astype(F32).sum(axis=0)
    decoded = (own_rows + mixed).astype(BF16)
    return (encoded.T, decoded)


def solution(mesh):
    in_specs = (
        P("dp", None),
        P("dp"),
        P(),
        P(),
        P(),
        P(None, "tensor"),
        P(None, "tensor"),
        P(None, "tensor"),
        P("tensor", None),
        P("dp", None),
        P("dp"),
        P(),
        P(),
        P(None, "tensor"),
        P(None, "tensor"),
        P(None, "tensor"),
        P("tensor", None),
    )
    out_specs = (P("dp", "tensor"), P(("dp", "tensor"), None))
    return jax.shard_map(body, mesh=mesh, in_specs=in_specs, out_specs=out_specs, check_vma=False)
```
